768 devices in a mesh: seq: 192 (over z, x, y_lo), tensor: 4 (over y_hi, core).
Axes of the slice: x: 4, y: 8 (y_hi: 2, y_lo: 4; y = y_hi * 4 + y_lo), z: 12, core: 2. Of those that a mesh axis runs over, the one named last changes fastest.
Arguments:
- query_rows: bfloat16 [24576, 2048], P('seq', 'tensor'), may hold values from -6 to 6
- key_rows: bfloat16 [24576, 2048], P('seq', 'tensor'), may hold values from -6 to 6
- value_rows: bfloat16 [24576, 2048], P('seq', 'tensor'), may hold values from -6 to 6
- w_out: bfloat16 [2048, 4096], P('tensor'), may hold values from -0.125 to 0.125
- d_out: bfloat16 [24576, 4096], P('seq', 'tensor'), may hold values from -6 to 6
Outputs:
- output: bfloat16 [24576, 4096], P('seq', 'tensor')
- d_queries: bfloat16 [24576, 2048], P('seq', 'tensor')
- d_keys: bfloat16 [24576, 2048], P('seq', 'tensor')
- d_values: bfloat16 [24576, 2048], P('seq', 'tensor')
The draws below stay inside these ranges and needn't reach their ends.
All inputs are finite; a program needn't handle non-finite values.
Results may differ from the reference program's by a relative error of at most 0.03225.
Values may be sent and summed in bfloat16 or wider, within the bound.
No kernel may reach another device: no remote copies, remote signals or barrier semaphores. Data moves between devices by JAX's collectives and lax.ppermute only.
A program may use at most 64 MiB of HBM per device.

```python
import math
import jax
import jax.numpy as jnp
from jax import lax

D = 4096
HEADS = 16
HD = 128
WINDOW = 2048
TOK_DEV = 128
HC = 2048
TOKENS = 24576
N_TENSOR = 4


def draw_query_rows(key, part):
    fresh_key = jax.random.fold_in(key, 11)
    drawn = jnp.clip(jax.random.normal(fresh_key, (TOKENS, HEADS * HD), jnp.float32), -4.0, 4.0)
    return drawn.astype(jnp.bfloat16)


def draw_key_rows(key, part):
    fresh_key = jax.random.fold_in(key, 21)
    scale_key = jax.random.fold_in(key, 31)
    row_scale = jnp.exp(jax.random.uniform(scale_key, (TOKENS, HEADS), jnp.float32, math.log(0.25), math.log(1.5)))
    row_scale = jnp.repeat(row_scale, HD, axis=1)
    drawn = jnp.clip(jax.random.normal(fresh_key, (TOKENS, HEADS * HD), jnp.float32), -3.0, 3.0) * row_scale
    return drawn.astype(jnp.bfloat16)


def steps_of(key, shape, cuts, low, high):
    def one(axis_at, blocks):
        draws = jax.random.uniform(jax.random.fold_in(jax.random.fold_in(key, 6), axis_at), (blocks,), jnp.float32, low / len(cuts), high / len(cuts))
        return jnp.repeat(jnp.exp(draws), shape[axis_at] // blocks).reshape((-1,) + (1,) * (len(shape) - axis_at - 1))

    level = one(*cuts[0])
    for cut in cuts[1:]:
        level = level * one(*cut)
    return level


def bell_draw(rng, dims, scale, reach, split=(), kind=jnp.bfloat16):
    drawn = jax.random.normal(rng, dims, jnp.float32) * scale
    if len(split) > 0:
        drawn = steps_of(rng, dims, split, -0.22, 0.18) * drawn
    return jnp.clip(drawn, min=-reach, max=reach).astype(kind)


def setup_inputs(seed: int = 0) -> dict:
    seeds = jax.random.split(jax.random.key(seed), 6)
    return {
        "query_rows": draw_query_rows(jax.random.fold_in(seeds[5], 71), 0),
        "key_rows": draw_key_rows(jax.random.fold_in(seeds[5], 71), 0),
        "value_rows": bell_draw(seeds[2], (TOKENS, HC), 1.0, 6.0, ((0, 192), (1, 4))),
        "w_out": bell_draw(seeds[3], (HC, D), HC ** -0.5, 0.125, ((0, 4),)),
        "d_out": bell_draw(seeds[4], (TOKENS, D), 1.0, 6.0, ((0, 192), (1, 4))),
    }


masked_score = -1e+30

def in_band(query_pos, key_pos, limit):
    return (key_pos[None, :] <= query_pos[:, None]) & (key_pos[None, :] > query_pos[:, None] - WINDOW) & (key_pos[None, :] >= 0) & (query_pos[:, None] < limit)

def reference(query_rows, key_rows, value_rows, w_out, d_out):
    scale = 1.0 / math.sqrt(HD)
    width = HEADS * HD
    block_len = TOK_DEV
    block_count = TOKENS // block_len
    zero_pad = jnp.zeros((WINDOW, width), jnp.bfloat16)
    keys_front = jnp.concatenate([zero_pad, key_rows], axis=0)
    values_front = jnp.concatenate([zero_pad, value_rows], axis=0)

    def front_window(index):
        start = index * block_len
        query_heads = lax.dynamic_slice_in_dim(query_rows, start, block_len, 0).reshape(block_len, HEADS, HD).astype(jnp.float32)
        key_heads = lax.dynamic_slice_in_dim(keys_front, start, WINDOW + block_len, 0).reshape(WINDOW + block_len, HEADS, HD).astype(jnp.float32)
        value_heads = lax.dynamic_slice_in_dim(values_front, start, WINDOW + block_len, 0).reshape(WINDOW + block_len, HEADS, HD).astype(jnp.float32)
        query_pos = start + jnp.arange(block_len, dtype=jnp.int32)
        key_pos = start - WINDOW + jnp.arange(WINDOW + block_len, dtype=jnp.int32)
        allowed = in_band(query_pos, key_pos, TOKENS)[None]
        scores = jnp.einsum('rhd,khd->hrk', query_heads, key_heads) * scale
        return (allowed, scores, key_heads, value_heads, start)

    def forward_block(index):
        allowed, scores, key_heads, value_heads, start = front_window(index)
        scores = jnp.where(allowed, scores, masked_score)
        row_max = lax.optimization_barrier(jnp.max(scores, axis=2, keepdims=True))
        log_total = row_max + jnp.log(lax.optimization_barrier(jnp.sum(jnp.exp(scores - row_max), axis=2, keepdims=True)))
        probs = jnp.where(allowed, jnp.exp(scores - log_total), 0.0)
        weights = probs.astype(jnp.bfloat16).astype(jnp.float32)
        attended_block = jnp.einsum('hrk,khd->rhd', weights, value_heads).astype(jnp.bfloat16)
        return (attended_block.reshape(block_len, width), log_total[:, :, 0])
    attended, log_totals = lax.map(forward_block, jnp.arange(block_count, dtype=jnp.int32))
    attended = attended.reshape(TOKENS, width)
    log_totals = jnp.transpose(log_totals, (1, 0, 2)).reshape(HEADS, TOKENS)
    group = width // N_TENSOR
    summed = jnp.zeros((TOKENS, D), jnp.float32)
    for group_no in range(N_TENSOR):
        part_term = jnp.dot(attended[:, group_no * group:(group_no + 1) * group], w_out[group_no * group:(group_no + 1) * group], preferred_element_type=jnp.float32)
        summed = summed + lax.optimization_barrier(part_term.astype(jnp.bfloat16)).astype(jnp.float32)
    output = summed.astype(jnp.bfloat16)
    d_attended = jnp.dot(d_out, w_out.T, preferred_element_type=jnp.float32).astype(jnp.bfloat16)
    delta = lax.optimization_barrier(jnp.sum((d_attended.astype(jnp.float32) * attended.astype(jnp.float32)).reshape(TOKENS, HEADS, HD), axis=2)).T

    def query_grad(index):
        allowed, scores, key_heads, value_heads, start = front_window(index)
        log_block = lax.dynamic_slice_in_dim(log_totals, start, block_len, 1)
        delta_block = lax.dynamic_slice_in_dim(delta, start, block_len, 1)
        probs = jnp.where(allowed, jnp.exp(scores - log_block[:, :, None]), 0.0)
        d_heads = lax.dynamic_slice_in_dim(d_attended, start, block_len, 0).reshape(block_len, HEADS, HD).astype(jnp.float32)
        d_probs = jnp.einsum('rhd,khd->hrk', d_heads, value_heads)
        d_scores = (scale * probs * (d_probs - delta_block[:, :, None])).astype(jnp.bfloat16).astype(jnp.float32)
        return jnp.einsum('hrk,khd->rhd', d_scores, key_heads).astype(jnp.bfloat16).reshape(block_len, width)
    d_queries = lax.map(query_grad, jnp.arange(block_count, dtype=jnp.int32)).reshape(TOKENS, width)
    queries_back = jnp.concatenate([query_rows, zero_pad], axis=0)
    d_back = jnp.concatenate([d_attended, zero_pad], axis=0)
    stat_pad = jnp.zeros((HEADS, WINDOW), jnp.float32)
    log_back = jnp.concatenate([log_totals, stat_pad], axis=1)
    delta_back = jnp.concatenate([delta, stat_pad], axis=1)

    def key_grad(index):
        start = index * block_len
        span_len = WINDOW + block_len
        key_heads = lax.dynamic_slice_in_dim(key_rows, start, block_len, 0).reshape(block_len, HEADS, HD).astype(jnp.float32)
        value_heads = lax.dynamic_slice_in_dim(value_rows, start, block_len, 0).reshape(block_len, HEADS, HD).astype(jnp.float32)
        later_q = lax.dynamic_slice_in_dim(queries_back, start, span_len, 0).reshape(span_len, HEADS, HD).astype(jnp.float32)
        later_d = lax.dynamic_slice_in_dim(d_back, start, span_len, 0).reshape(span_len, HEADS, HD).astype(jnp.float32)
        later_log = lax.dynamic_slice_in_dim(log_back, start, span_len, 1)
        later_delta = lax.dynamic_slice_in_dim(delta_back, start, span_len, 1)
        query_pos = start + jnp.arange(span_len, dtype=jnp.int32)
        key_pos = start + jnp.arange(block_len, dtype=jnp.int32)
        allowed = in_band(query_pos, key_pos, TOKENS)[None]
        scores = jnp.einsum('qhd,khd->hqk', later_q, key_heads) * scale
        probs = jnp.where(allowed, jnp.exp(scores - later_log[:, :, None]), 0.0)
        d_probs = jnp.einsum('qhd,khd->hqk', later_d, value_heads)
        d_scores = (scale * probs * (d_probs - later_delta[:, :, None])).astype(jnp.bfloat16).astype(jnp.float32)
        weights = probs.astype(jnp.bfloat16).astype(jnp.float32)
        d_key_block = jnp.einsum('hqk,qhd->khd', d_scores, later_q).astype(jnp.bfloat16)
        d_value_block = jnp.einsum('hqk,qhd->khd', weights, later_d).astype(jnp.bfloat16)
        return (d_key_block.reshape(block_len, width), d_value_block.reshape(block_len, width))
    d_keys, d_values = lax.map(key_grad, jnp.arange(block_count, dtype=jnp.int32))
    return (output, d_queries, d_keys.reshape(TOKENS, width), d_values.reshape(TOKENS, width))
```

```python
import math

import jax
import jax.numpy as jnp
from jax import lax
from jax.sharding import Mesh
from jax.sharding import PartitionSpec as P

HD = 128
WINDOW = 2048


masked_score = -1e30


def shifted(block, axis, distance):
    devices = range(lax.axis_size(axis))
    route = [(i - distance, i) for i in devices if i - distance in devices]
    return lax.ppermute(block, axis, route)


def in_band(query_pos, key_pos, limit):
    return (
        (key_pos[None, :] <= query_pos[:, None])
        & (key_pos[None, :] > query_pos[:, None] - WINDOW)
        & (key_pos[None, :] >= 0)
        & (query_pos[:, None] < limit)
    )


def body(query_rows, key_rows, value_rows, w_out, d_out):
    tok_rows, col_dev = query_rows.shape
    n_grp = lax.axis_size("grp")
    n_sub = lax.axis_size("sub")
    my_grp = lax.axis_index("grp")
    blk = tok_rows * n_sub
    reach = min(-(-WINDOW // blk), n_grp - 1)
    span_len = (reach + 1) * blk
    scale = 1.0 / math.sqrt(HD)
    limit = blk * n_grp

    qkv = lax.all_to_all(
        jnp.stack([query_rows, key_rows, value_rows]), "sub", 2, 1, tiled=True
    )
    q_h, k_h, v_h = qkv[0], qkv[1], qkv[2]

    kv = jnp.stack([k_h, v_h])
    pieces = [shifted(kv, "grp", m) for m in range(reach, 0, -1)] + [kv]
    kv_span = jnp.concatenate(pieces, axis=1)
    key_span, value_span = kv_span[0], kv_span[1]

    own_pos = my_grp * blk + jnp.arange(blk, dtype=jnp.int32)
    key_pos = (my_grp - reach) * blk + jnp.arange(span_len, dtype=jnp.int32)
    allowed = in_band(own_pos, key_pos, limit)
    scores = (
        jnp.einsum("rd,kd->rk", q_h, key_span, preferred_element_type=jnp.float32) * scale
    )
    scores = jnp.where(allowed, scores, masked_score)
    row_max = jnp.max(scores, axis=1, keepdims=True)
    log_total = row_max + jnp.log(jnp.sum(jnp.exp(scores - row_max), axis=1, keepdims=True))
    probs = jnp.where(allowed, jnp.exp(scores - log_total), 0.0)
    weights = probs.astype(jnp.bfloat16)
    att_h = jnp.einsum(
        "rk,kd->rd", weights, value_span, preferred_element_type=jnp.float32
    ).astype(jnp.bfloat16)

    attended = lax.all_to_all(att_h, "sub", 0, 1, tiled=True)
    partial_out = jnp.dot(attended, w_out, preferred_element_type=jnp.float32)
    output = lax.psum_scatter(
        partial_out.astype(jnp.bfloat16), "tensor", scatter_dimension=1, tiled=True
    )

    d_attended = lax.dot_general(
        lax.all_gather(d_out, "tensor", axis=1, tiled=True),
        w_out,
        (((1,), (1,)), ((), ())),
        preferred_element_type=jnp.float32,
    ).astype(jnp.bfloat16)
    d_h = lax.all_to_all(d_attended, "sub", 1, 0, tiled=True)
    delta = jnp.sum(d_h.astype(jnp.float32) * att_h.astype(jnp.float32), axis=1)

    d_probs = jnp.einsum("rd,kd->rk", d_h, value_span, preferred_element_type=jnp.float32)
    d_scores = (scale * probs * (d_probs - delta[:, None])).astype(jnp.bfloat16)
    dq_h = jnp.einsum(
        "rk,kd->rd", d_scores, key_span, preferred_element_type=jnp.float32
    ).astype(jnp.bfloat16)

    pair = jnp.stack([q_h, d_h])
    stats = jnp.stack([log_total[:, 0], delta])
    pair_span = jnp.concatenate(
        [pair] + [shifted(pair, "grp", -m) for m in range(1, reach + 1)], axis=1
    )
    stat_span = jnp.concatenate(
        [stats] + [shifted(stats, "grp", -m) for m in range(1, reach + 1)], axis=1
    )
    later_q, later_d = pair_span[0], pair_span[1]
    later_pos = my_grp * blk + jnp.arange(span_len, dtype=jnp.int32)
    allowed_back = in_band(later_pos, own_pos, limit)
    scores_back = (
        jnp.einsum("qd,kd->qk", later_q, k_h, preferred_element_type=jnp.float32) * scale
    )
    probs_back = jnp.where(allowed_back, jnp.exp(scores_back - stat_span[0][:, None]), 0.0)
    d_probs_back = jnp.einsum("qd,kd->qk", later_d, v_h, preferred_element_type=jnp.float32)
    d_scores_back = (scale * probs_back * (d_probs_back - stat_span[1][:, None])).astype(
        jnp.bfloat16
    )
    dk_h = jnp.einsum(
        "qk,qd->kd", d_scores_back, later_q, preferred_element_type=jnp.float32
    ).astype(jnp.bfloat16)
    dv_h = jnp.einsum(
        "qk,qd->kd", probs_back.astype(jnp.bfloat16), later_d, preferred_element_type=jnp.float32
    ).astype(jnp.bfloat16)

    grads = lax.all_to_all(jnp.stack([dq_h, dk_h, dv_h]), "sub", 1, 2, tiled=True)
    return (output, grads[0], grads[1], grads[2])


def solution(mesh):
    n_seq, n_tensor = mesh.devices.shape
    heads_dev = 2048 // HD // n_tensor
    regrouped = Mesh(
        mesh.devices.reshape(n_seq // heads_dev, heads_dev, n_tensor), ("grp", "sub", "tensor")
    )
    rows = P(("grp", "sub"), "tensor")
    placed = (rows, rows, rows, P("tensor", None), rows)
    return jax.shard_map(
        body,
        mesh=regrouped,
        in_specs=placed,
        out_specs=(rows, rows, rows, rows),
        check_vma=False,
    )
```

```python
import math

import jax
import jax.numpy as jnp
from jax import lax
from jax.sharding import Mesh
from jax.sharding import PartitionSpec as P

HD = 128
WINDOW = 2048


masked_score = -1e30


def shifted(block, axis, distance):
    devices = range(lax.axis_size(axis))
    route = [(i - distance, i) for i in devices if i - distance in devices]
    return lax.ppermute(block, axis, route)


def in_band(query_pos, key_pos, limit):
    return (
        (key_pos[None, :] <= query_pos[:, None])
        & (key_pos[None, :] > query_pos[:, None] - WINDOW)
        & (key_pos[None, :] >= 0)
        & (query_pos[:, None] < limit)
    )


def body(query_rows, key_rows, value_rows, w_out, d_out):
    tok_rows, col_dev = query_rows.shape
    n_grp = lax.axis_size("grp")
    n_sub = lax.axis_size("sub")
    my_grp = lax.axis_index("grp")
    blk = tok_rows * n_sub
    reach = min(-(-WINDOW // blk), n_grp - 1)
    span_len = (reach + 1) * blk
    scale = 1.0 / math.sqrt(HD)
    limit = blk * n_grp

    qkv = lax.all_to_all(
        jnp.stack([query_rows, key_rows, value_rows]), "sub", 2, 1, tiled=True
    )
    q_h, k_h, v_h = qkv[0], qkv[1], qkv[2]

    kv = jnp.stack([k_h, v_h])
    pieces = [shifted(kv, "grp", m) for m in range(reach, 0, -1)] + [kv]
    kv_span = jnp.concatenate(pieces, axis=1)
    key_span, value_span = kv_span[0], kv_span[1]

    own_pos = my_grp * blk + jnp.arange(blk, dtype=jnp.int32)
    key_pos = (my_grp - reach) * blk + jnp.arange(span_len, dtype=jnp.int32)
    allowed = in_band(own_pos, key_pos, limit)
    scores = (
        jnp.einsum("rd,kd->rk", q_h, key_span, preferred_element_type=jnp.float32) * scale
    )
    scores = jnp.where(allowed, scores, masked_score)
    row_max = jnp.max(scores, axis=1, keepdims=True)
    log_total = row_max + jnp.log(jnp.sum(jnp.exp(scores - row_max), axis=1, keepdims=True))
    probs = jnp.where(allowed, jnp.exp(scores - log_total), 0.0)
    weights = probs.astype(jnp.bfloat16)
    att_h = jnp.einsum(
        "rk,kd->rd", weights, value_span, preferred_element_type=jnp.float32
    ).astype(jnp.bfloat16)

    attended = lax.all_to_all(att_h, "sub", 0, 1, tiled=True)
    partial_out = jnp.dot(attended, w_out, preferred_element_type=jnp.float32)
    n_tensor = lax.axis_size("tensor")
    parts = partial_out.astype(jnp.bfloat16).reshape(tok_rows, n_tensor, -1)
    parts = lax.all_to_all(jnp.moveaxis(parts, 1, 0), "tensor", 0, 0)
    output = jnp.sum(parts.astype(jnp.float32), axis=0).astype(jnp.bfloat16)

    d_attended = lax.dot_general(
        lax.all_gather(d_out, "tensor", axis=1, tiled=True),
        w_out,
        (((1,), (1,)), ((), ())),
        preferred_element_type=jnp.float32,
    ).astype(jnp.bfloat16)
    d_h = lax.all_to_all(d_attended, "sub", 1, 0, tiled=True)
    delta = jnp.sum(d_h.astype(jnp.float32) * att_h.astype(jnp.float32), axis=1)

    d_probs = jnp.einsum("rd,kd->rk", d_h, value_span, preferred_element_type=jnp.float32)
    d_scores = (scale * probs * (d_probs - delta[:, None])).astype(jnp.bfloat16)
    dq_h = jnp.einsum(
        "rk,kd->rd", d_scores, key_span, preferred_element_type=jnp.float32
    ).astype(jnp.bfloat16)

    pair = jnp.stack([q_h, d_h])
    stats = jnp.stack([log_total[:, 0], delta])
    pair_span = jnp.concatenate(
        [pair] + [shifted(pair, "grp", -m) for m in range(1, reach + 1)], axis=1
    )
    stat_span = jnp.concatenate(
        [stats] + [shifted(stats, "grp", -m) for m in range(1, reach + 1)], axis=1
    )
    later_q, later_d = pair_span[0], pair_span[1]
    later_pos = my_grp * blk + jnp.arange(span_len, dtype=jnp.int32)
    allowed_back = in_band(later_pos, own_pos, limit)
    scores_back = (
        jnp.einsum("qd,kd->qk", later_q, k_h, preferred_element_type=jnp.float32) * scale
    )
    probs_back = jnp.where(allowed_back, jnp.exp(scores_back - stat_span[0][:, None]), 0.0)
    d_probs_back = jnp.einsum("qd,kd->qk", later_d, v_h, preferred_element_type=jnp.float32)
    d_scores_back = (scale * probs_back * (d_probs_back - stat_span[1][:, None])).astype(
        jnp.bfloat16
    )
    dk_h = jnp.einsum(
        "qk,qd->kd", d_scores_back, later_q, preferred_element_type=jnp.float32
    ).astype(jnp.bfloat16)
    dv_h = jnp.einsum(
        "qk,qd->kd", probs_back.astype(jnp.bfloat16), later_d, preferred_element_type=jnp.float32
    ).astype(jnp.bfloat16)

    grads = lax.all_to_all(jnp.stack([dq_h, dk_h, dv_h]), "sub", 1, 2, tiled=True)
    return (output, grads[0], grads[1], grads[2])


def solution(mesh):
    n_seq, n_tensor = mesh.devices.shape
    heads_dev = 2048 // HD // n_tensor
    regrouped = Mesh(
        mesh.devices.reshape(n_seq // heads_dev, heads_dev, n_tensor), ("grp", "sub", "tensor")
    )
    rows = P(("grp", "sub"), "tensor")
    placed = (rows, rows, rows, P("tensor", None), rows)
    return jax.shard_map(
        body,
        mesh=regrouped,
        in_specs=placed,
        out_specs=(rows, rows, rows, rows),
        check_vma=False,
    )
```

```python
import math

import jax
import jax.numpy as jnp
from jax import lax
from jax.sharding import Mesh
from jax.sharding import PartitionSpec as P

HD = 128
WINDOW = 2048


masked_score = -1e30


def shifted(block, axis, distance):
    devices = range(lax.axis_size(axis))
    route = [(i - distance, i) for i in devices if i - distance in devices]
    return lax.ppermute(block, axis, route)


def in_band(query_pos, key_pos, limit):
    return (
        (key_pos[None, :] <= query_pos[:, None])
        & (key_pos[None, :] > query_pos[:, None] - WINDOW)
        & (key_pos[None, :] >= 0)
        & (query_pos[:, None] < limit)
    )


def body(query_rows, key_rows, value_rows, w_out, d_out):
    tok_rows, col_dev = query_rows.shape
    n_grp = lax.axis_size("grp")
    n_sub = lax.axis_size("sub")
    my_grp = lax.axis_index("grp")
    blk = tok_rows * n_sub
    reach = min(-(-WINDOW // blk), n_grp - 1)
    span_len = (reach + 1) * blk
    scale = 1.0 / math.sqrt(HD)
    limit = blk * n_grp

    qkv = lax.all_to_all(
        jnp.stack([query_rows, key_rows, value_rows]), "sub", 2, 1, tiled=True
    )
    q_h, k_h, v_h = qkv[0], qkv[1], qkv[2]

    kv = jnp.stack([k_h, v_h])
    pieces = [shifted(kv, "grp", m) for m in range(reach, 0, -1)] + [kv]
    kv_span = jnp.concatenate(pieces, axis=1)
    key_span, value_span = kv_span[0], kv_span[1]

    own_pos = my_grp * blk + jnp.arange(blk, dtype=jnp.int32)
    key_pos = (my_grp - reach) * blk + jnp.arange(span_len, dtype=jnp.int32)
    allowed = in_band(own_pos, key_pos, limit)
    scores = (
        jnp.einsum("rd,kd->rk", q_h, key_span, preferred_element_type=jnp.float32) * scale
    )
    scores = jnp.where(allowed, scores, masked_score)
    row_max = jnp.max(scores, axis=1, keepdims=True)
    log_total = row_max + jnp.log(jnp.sum(jnp.exp(scores - row_max), axis=1, keepdims=True))
    probs = jnp.where(allowed, jnp.exp(scores - log_total), 0.0)
    weights = probs.astype(jnp.bfloat16)
    att_h = jnp.einsum(
        "rk,kd->rd", weights, value_span, preferred_element_type=jnp.float32
    ).astype(jnp.bfloat16)

    attended = lax.all_to_all(att_h, "sub", 0, 1, tiled=True)
    partial_out = jnp.dot(attended, w_out, preferred_element_type=jnp.float32)
    n_tensor = lax.axis_size("tensor")
    my_t = lax.axis_index("tensor")
    my_core = my_t % 2
    my_hi = my_t // 2
    parts = partial_out.astype(jnp.bfloat16).reshape(tok_rows, n_tensor // 2, 2, -1)
    keep = lax.dynamic_index_in_dim(parts, my_core, 2, keepdims=False)
    send = lax.dynamic_index_in_dim(parts, 1 - my_core, 2, keepdims=False)
    got = lax.ppermute(send, "tensor", [(t, t ^ 1) for t in range(n_tensor)])
    chip_sum = keep.astype(jnp.float32) + got.astype(jnp.float32)
    mine = lax.dynamic_index_in_dim(chip_sum, my_hi, 1, keepdims=False)
    other = lax.dynamic_index_in_dim(chip_sum, 1 - my_hi, 1, keepdims=False)
    got2 = lax.ppermute(
        other.astype(jnp.bfloat16), "tensor", [(t, t ^ 2) for t in range(n_tensor)]
    )
    output = (mine + got2.astype(jnp.float32)).astype(jnp.bfloat16)

    d_attended = lax.dot_general(
        lax.all_gather(d_out, "tensor", axis=1, tiled=True),
        w_out,
        (((1,), (1,)), ((), ())),
        preferred_element_type=jnp.float32,
    ).astype(jnp.bfloat16)
    d_h = lax.all_to_all(d_attended, "sub", 1, 0, tiled=True)
    delta = jnp.sum(d_h.astype(jnp.float32) * att_h.astype(jnp.float32), axis=1)

    d_probs = jnp.einsum("rd,kd->rk", d_h, value_span, preferred_element_type=jnp.float32)
    d_scores = (scale * probs * (d_probs - delta[:, None])).astype(jnp.bfloat16)
    dq_h = jnp.einsum(
        "rk,kd->rd", d_scores, key_span, preferred_element_type=jnp.float32
    ).astype(jnp.bfloat16)
    d_queries = lax.all_to_all(dq_h, "sub", 0, 1, tiled=True)

    pair = jnp.stack([q_h, d_h])
    stats = jnp.stack([log_total[:, 0], delta])
    pair_span = jnp.concatenate(
        [pair] + [shifted(pair, "grp", -m) for m in range(1, reach + 1)], axis=1
    )
    stat_span = jnp.concatenate(
        [stats] + [shifted(stats, "grp", -m) for m in range(1, reach + 1)], axis=1
    )
    later_q, later_d = pair_span[0], pair_span[1]
    later_pos = my_grp * blk + jnp.arange(span_len, dtype=jnp.int32)
    allowed_back = in_band(later_pos, own_pos, limit)
    scores_back = (
        jnp.einsum("qd,kd->qk", later_q, k_h, preferred_element_type=jnp.float32) * scale
    )
    probs_back = jnp.where(allowed_back, jnp.exp(scores_back - stat_span[0][:, None]), 0.0)
    d_probs_back = jnp.einsum("qd,kd->qk", later_d, v_h, preferred_element_type=jnp.float32)
    d_scores_back = (scale * probs_back * (d_probs_back - stat_span[1][:, None])).astype(
        jnp.bfloat16
    )
    dk_h = jnp.einsum(
        "qk,qd->kd", d_scores_back, later_q, preferred_element_type=jnp.float32
    ).astype(jnp.bfloat16)
    dv_h = jnp.einsum(
        "qk,qd->kd", probs_back.astype(jnp.bfloat16), later_d, preferred_element_type=jnp.float32
    ).astype(jnp.bfloat16)

    grads = lax.all_to_all(jnp.stack([dk_h, dv_h]), "sub", 1, 2, tiled=True)
    return (output, d_queries, grads[0], grads[1])


def solution(mesh):
    n_seq, n_tensor = mesh.devices.shape
    heads_dev = 2048 // HD // n_tensor
    regrouped = Mesh(
        mesh.devices.reshape(n_seq // heads_dev, heads_dev, n_tensor), ("grp", "sub", "tensor")
    )
    rows = P(("grp", "sub"), "tensor")
    placed = (rows, rows, rows, P("tensor", None), rows)
    return jax.shard_map(
        body,
        mesh=regrouped,
        in_specs=placed,
        out_specs=(rows, rows, rows, rows),
        check_vma=False,
    )
```

```python
import math

import jax
import jax.numpy as jnp
from jax import lax
from jax.sharding import Mesh
from jax.sharding import PartitionSpec as P

HD = 128
WINDOW = 2048


masked_score = -1e30


def shifted(block, axis, distance):
    devices = range(lax.axis_size(axis))
    route = [(i - distance, i) for i in devices if i - distance in devices]
    return lax.ppermute(block, axis, route)


def in_band(query_pos, key_pos, limit):
    return (
        (key_pos[None, :] <= query_pos[:, None])
        & (key_pos[None, :] > query_pos[:, None] - WINDOW)
        & (key_pos[None, :] >= 0)
        & (query_pos[:, None] < limit)
    )


def body(query_rows, key_rows, value_rows, w_out, d_out):
    tok_rows, col_dev = query_rows.shape
    n_grp = lax.axis_size("grp")
    n_sub = lax.axis_size("sub")
    my_grp = lax.axis_index("grp")
    blk = tok_rows * n_sub
    reach = min(-(-WINDOW // blk), n_grp - 1)
    span_len = (reach + 1) * blk
    scale = 1.0 / math.sqrt(HD)
    limit = blk * n_grp

    qkv = lax.all_to_all(
        jnp.stack([query_rows, key_rows, value_rows]), "sub", 2, 1, tiled=True
    )
    q_h, k_h, v_h = qkv[0], qkv[1], qkv[2]

    kv = jnp.stack([k_h, v_h])
    pieces = [shifted(kv, "grp", m) for m in range(reach, 0, -1)] + [kv]
    kv_span = jnp.concatenate(pieces, axis=1)
    key_span, value_span = kv_span[0], kv_span[1]

    own_pos = my_grp * blk + jnp.arange(blk, dtype=jnp.int32)
    key_pos = (my_grp - reach) * blk + jnp.arange(span_len, dtype=jnp.int32)
    allowed = in_band(own_pos, key_pos, limit)
    scores = (
        jnp.einsum("rd,kd->rk", q_h, key_span, preferred_element_type=jnp.float32) * scale
    )
    scores = jnp.where(allowed, scores, masked_score)
    row_max = jnp.max(scores, axis=1, keepdims=True)
    log_total = row_max + jnp.log(jnp.sum(jnp.exp(scores - row_max), axis=1, keepdims=True))
    probs = jnp.where(allowed, jnp.exp(scores - log_total), 0.0)
    weights = probs.astype(jnp.bfloat16)
    att_h = jnp.einsum(
        "rk,kd->rd", weights, value_span, preferred_element_type=jnp.float32
    ).astype(jnp.bfloat16)

    attended = lax.all_to_all(att_h, "sub", 0, 1, tiled=True)
    partial_out = jnp.dot(attended, w_out, preferred_element_type=jnp.float32)
    n_tensor = lax.axis_size("tensor")
    my_t = lax.axis_index("tensor")
    my_core = my_t % 2
    my_hi = my_t // 2
    parts = partial_out.astype(jnp.bfloat16).reshape(tok_rows, n_tensor // 2, 2, -1)
    keep = lax.dynamic_index_in_dim(parts, my_core, 2, keepdims=False)
    send = lax.dynamic_index_in_dim(parts, 1 - my_core, 2, keepdims=False)
    got = lax.ppermute(send, "tensor", [(t, t ^ 1) for t in range(n_tensor)])
    chip_sum = keep.astype(jnp.float32) + got.astype(jnp.float32)
    mine = lax.dynamic_index_in_dim(chip_sum, my_hi, 1, keepdims=False)
    other = lax.dynamic_index_in_dim(chip_sum, 1 - my_hi, 1, keepdims=False)
    got2 = lax.ppermute(
        other.astype(jnp.bfloat16), "tensor", [(t, t ^ 2) for t in range(n_tensor)]
    )
    output = (mine + got2.astype(jnp.float32)).astype(jnp.bfloat16)

    far = lax.ppermute(d_out, "tensor", [(t, t ^ 2) for t in range(n_tensor)])
    near = lax.ppermute(
        jnp.stack([d_out, far]), "tensor", [(t, t ^ 1) for t in range(n_tensor)]
    )
    by_xor = jnp.stack([d_out, near[0], far, near[1]])
    order = jnp.arange(n_tensor, dtype=jnp.int32) ^ my_t
    d_out_full = jnp.moveaxis(jnp.take(by_xor, order, axis=0), 0, 1).reshape(tok_rows, -1)
    d_attended = lax.dot_general(
        d_out_full,
        w_out,
        (((1,), (1,)), ((), ())),
        preferred_element_type=jnp.float32,
    ).astype(jnp.bfloat16)
    d_h = lax.all_to_all(d_attended, "sub", 1, 0, tiled=True)
    delta = jnp.sum(d_h.astype(jnp.float32) * att_h.astype(jnp.float32), axis=1)

    d_probs = jnp.einsum("rd,kd->rk", d_h, value_span, preferred_element_type=jnp.float32)
    d_scores = (scale * probs * (d_probs - delta[:, None])).astype(jnp.bfloat16)
    dq_h = jnp.einsum(
        "rk,kd->rd", d_scores, key_span, preferred_element_type=jnp.float32
    ).astype(jnp.bfloat16)
    d_queries = lax.all_to_all(dq_h, "sub", 0, 1, tiled=True)

    pair = jnp.stack([q_h, d_h])
    stats = jnp.stack([log_total[:, 0], delta])
    pair_span = jnp.concatenate(
        [pair] + [shifted(pair, "grp", -m) for m in range(1, reach + 1)], axis=1
    )
    stat_span = jnp.concatenate(
        [stats] + [shifted(stats, "grp", -m) for m in range(1, reach + 1)], axis=1
    )
    later_q, later_d = pair_span[0], pair_span[1]
    later_pos = my_grp * blk + jnp.arange(span_len, dtype=jnp.int32)
    allowed_back = in_band(later_pos, own_pos, limit)
    scores_back = (
        jnp.einsum("qd,kd->qk", later_q, k_h, preferred_element_type=jnp.float32) * scale
    )
    probs_back = jnp.where(allowed_back, jnp.exp(scores_back - stat_span[0][:, None]), 0.0)
    d_probs_back = jnp.einsum("qd,kd->qk", later_d, v_h, preferred_element_type=jnp.float32)
    d_scores_back = (scale * probs_back * (d_probs_back - stat_span[1][:, None])).astype(
        jnp.bfloat16
    )
    dk_h = jnp.einsum(
        "qk,qd->kd", d_scores_back, later_q, preferred_element_type=jnp.float32
    ).astype(jnp.bfloat16)
    dv_h = jnp.einsum(
        "qk,qd->kd", probs_back.astype(jnp.bfloat16), later_d, preferred_element_type=jnp.float32
    ).astype(jnp.bfloat16)

    grads = lax.all_to_all(jnp.stack([dk_h, dv_h]), "sub", 1, 2, tiled=True)
    return (output, d_queries, grads[0], grads[1])


def solution(mesh):
    n_seq, n_tensor = mesh.devices.shape
    heads_dev = 2048 // HD // n_tensor
    regrouped = Mesh(
        mesh.devices.reshape(n_seq // heads_dev, heads_dev, n_tensor), ("grp", "sub", "tensor")
    )
    rows = P(("grp", "sub"), "tensor")
    placed = (rows, rows, rows, P("tensor", None), rows)
    return jax.shard_map(
        body,
        mesh=regrouped,
        in_specs=placed,
        out_specs=(rows, rows, rows, rows),
        check_vma=False,
    )
```

```python
import math

import jax
import jax.numpy as jnp
from jax import lax
from jax.sharding import Mesh
from jax.sharding import PartitionSpec as P

HD = 128
WINDOW = 2048


masked_score = -1e30


def shifted(block, axis, distance):
    devices = range(lax.axis_size(axis))
    route = [(i - distance, i) for i in devices if i - distance in devices]
    return lax.ppermute(block, axis, route)


def in_band(query_pos, key_pos, limit):
    return (
        (key_pos[None, :] <= query_pos[:, None])
        & (key_pos[None, :] > query_pos[:, None] - WINDOW)
        & (key_pos[None, :] >= 0)
        & (query_pos[:, None] < limit)
    )


def body(query_rows, key_rows, value_rows, w_out, d_out):
    tok_rows, col_dev = query_rows.shape
    n_grp = lax.axis_size("grp")
    n_sub = lax.axis_size("sub")
    my_grp = lax.axis_index("grp")
    blk = tok_rows * n_sub
    reach = min(-(-WINDOW // blk), n_grp - 1)
    span_len = (reach + 1) * blk
    scale = 1.0 / math.sqrt(HD)
    limit = blk * n_grp

    qkv = lax.all_to_all(
        jnp.stack([query_rows, key_rows, value_rows]), "sub", 2, 1, tiled=True
    )
    q_h, k_h, v_h = qkv[0], qkv[1], qkv[2]

    kv = jnp.stack([k_h, v_h])
    pieces = [shifted(kv, "grp", m) for m in range(reach, 0, -1)] + [kv]
    kv_span = jnp.concatenate(pieces, axis=1)
    key_span, value_span = kv_span[0], kv_span[1]

    own_pos = my_grp * blk + jnp.arange(blk, dtype=jnp.int32)
    key_pos = (my_grp - reach) * blk + jnp.arange(span_len, dtype=jnp.int32)
    allowed = in_band(own_pos, key_pos, limit)
    scores = (
        jnp.einsum("rd,kd->rk", q_h, key_span, preferred_element_type=jnp.float32) * scale
    )
    scores = jnp.where(allowed, scores, masked_score)
    row_max = jnp.max(scores, axis=1, keepdims=True)
    log_total = row_max + jnp.log(jnp.sum(jnp.exp(scores - row_max), axis=1, keepdims=True))
    probs = jnp.where(allowed, jnp.exp(scores - log_total), 0.0)
    weights = probs.astype(jnp.bfloat16)
    att_h = jnp.einsum(
        "rk,kd->rd", weights, value_span, preferred_element_type=jnp.float32
    ).astype(jnp.bfloat16)

    attended = lax.all_to_all(att_h, "sub", 0, 1, tiled=True)
    partial_out = jnp.dot(attended, w_out, preferred_element_type=jnp.float32)
    n_tensor = lax.axis_size("tensor")
    my_t = lax.axis_index("tensor")
    my_core = my_t % 2
    my_hi = my_t // 2
    parts = partial_out.astype(jnp.bfloat16).reshape(tok_rows, n_tensor // 2, 2, -1)
    keep = lax.dynamic_index_in_dim(parts, my_core, 2, keepdims=False)
    send = lax.dynamic_index_in_dim(parts, 1 - my_core, 2, keepdims=False)
    got = lax.ppermute(send, "tensor", [(t, t ^ 1) for t in range(n_tensor)])
    chip_sum = keep.astype(jnp.float32) + got.astype(jnp.float32)
    mine = lax.dynamic_index_in_dim(chip_sum, my_hi, 1, keepdims=False)
    other = lax.dynamic_index_in_dim(chip_sum, 1 - my_hi, 1, keepdims=False)
    got2 = lax.ppermute(
        other.astype(jnp.bfloat16), "tensor", [(t, t ^ 2) for t in range(n_tensor)]
    )
    output = (mine + got2.astype(jnp.float32)).astype(jnp.bfloat16)

    far = lax.ppermute(d_out, "tensor", [(t, t ^ 2) for t in range(n_tensor)])
    near = lax.ppermute(
        jnp.stack([d_out, far]), "tensor", [(t, t ^ 1) for t in range(n_tensor)]
    )
    by_xor = jnp.stack([d_out, near[0], far, near[1]])
    order = jnp.arange(n_tensor, dtype=jnp.int32) ^ my_t
    d_out_full = jnp.moveaxis(jnp.take(by_xor, order, axis=0), 0, 1).reshape(tok_rows, -1)
    d_attended = lax.dot_general(
        d_out_full,
        w_out,
        (((1,), (1,)), ((), ())),
        preferred_element_type=jnp.float32,
    ).astype(jnp.bfloat16)
    d_h = lax.all_to_all(d_attended, "sub", 1, 0, tiled=True)
    delta = jnp.sum(d_h.astype(jnp.float32) * att_h.astype(jnp.float32), axis=1)

    d_probs = jnp.einsum("rd,kd->rk", d_h, value_span, preferred_element_type=jnp.float32)
    d_scores = (scale * probs * (d_probs - delta[:, None])).astype(jnp.bfloat16)
    dq_h = jnp.einsum(
        "rk,kd->rd", d_scores, key_span, preferred_element_type=jnp.float32
    ).astype(jnp.bfloat16)
    d_queries = lax.all_to_all(dq_h, "sub", 0, 1, tiled=True)

    pair = jnp.stack([q_h, d_h])
    stats = jnp.stack([log_total[:, 0], delta])
    hi = lax.reduce_precision(stats, exponent_bits=8, mantissa_bits=7)
    rest = stats - hi
    mid = lax.reduce_precision(rest, exponent_bits=8, mantissa_bits=7)
    lo = rest - mid
    split = jnp.concatenate([hi, mid, lo]).astype(jnp.bfloat16)
    n_stat_rows = split.size // HD
    packed = jnp.concatenate(
        [pair.reshape(-1, HD), split.reshape(n_stat_rows, HD)], axis=0
    )
    pair_pieces = [pair]
    stat_pieces = [stats]
    for m in range(1, reach + 1):
        got = shifted(packed, "grp", -m)
        pair_pieces.append(got[: pair.size // HD].reshape(pair.shape))
        parts3 = got[pair.size // HD :].reshape(3, 2, blk).astype(jnp.float32)
        stat_pieces.append((parts3[0] + parts3[1]) + parts3[2])
    pair_span = jnp.concatenate(pair_pieces, axis=1)
    stat_span = jnp.concatenate(stat_pieces, axis=1)
    later_q, later_d = pair_span[0], pair_span[1]
    later_pos = my_grp * blk + jnp.arange(span_len, dtype=jnp.int32)
    allowed_back = in_band(later_pos, own_pos, limit)
    scores_back = (
        jnp.einsum("qd,kd->qk", later_q, k_h, preferred_element_type=jnp.float32) * scale
    )
    probs_back = jnp.where(allowed_back, jnp.exp(scores_back - stat_span[0][:, None]), 0.0)
    d_probs_back = jnp.einsum("qd,kd->qk", later_d, v_h, preferred_element_type=jnp.float32)
    d_scores_back = (scale * probs_back * (d_probs_back - stat_span[1][:, None])).astype(
        jnp.bfloat16
    )
    dk_h = jnp.einsum(
        "qk,qd->kd", d_scores_back, later_q, preferred_element_type=jnp.float32
    ).astype(jnp.bfloat16)
    dv_h = jnp.einsum(
        "qk,qd->kd", probs_back.astype(jnp.bfloat16), later_d, preferred_element_type=jnp.float32
    ).astype(jnp.bfloat16)

    grads = lax.all_to_all(jnp.stack([dk_h, dv_h]), "sub", 1, 2, tiled=True)
    return (output, d_queries, grads[0], grads[1])


def solution(mesh):
    n_seq, n_tensor = mesh.devices.shape
    heads_dev = 2048 // HD // n_tensor
    regrouped = Mesh(
        mesh.devices.reshape(n_seq // heads_dev, heads_dev, n_tensor), ("grp", "sub", "tensor")
    )
    rows = P(("grp", "sub"), "tensor")
    placed = (rows, rows, rows, P("tensor", None), rows)
    return jax.shard_map(
        body,
        mesh=regrouped,
        in_specs=placed,
        out_specs=(rows, rows, rows, rows),
        check_vma=False,
    )
```

```python
import math

import jax
import jax.numpy as jnp
from jax import lax
from jax.sharding import Mesh
from jax.sharding import PartitionSpec as P

HD = 128
WINDOW = 2048


masked_score = -1e30


def shifted(block, axis, distance):
    devices = range(lax.axis_size(axis))
    route = [(i - distance, i) for i in devices if i - distance in devices]
    return lax.ppermute(block, axis, route)


def in_band(query_pos, key_pos, limit):
    return (
        (key_pos[None, :] <= query_pos[:, None])
        & (key_pos[None, :] > query_pos[:, None] - WINDOW)
        & (key_pos[None, :] >= 0)
        & (query_pos[:, None] < limit)
    )


def body(query_rows, key_rows, value_rows, w_out, d_out):
    tok_rows, col_dev = query_rows.shape
    n_grp = lax.axis_size("grp")
    n_sub = lax.axis_size("sub")
    my_grp = lax.axis_index("grp")
    blk = tok_rows * n_sub
    reach = min(-(-WINDOW // blk), n_grp - 1)
    span_len = (reach + 1) * blk
    scale = 1.0 / math.sqrt(HD)
    limit = blk * n_grp
    n_tensor = lax.axis_size("tensor")
    my_t = lax.axis_index("tensor")

    qkv = lax.all_to_all(
        jnp.stack([query_rows, key_rows, value_rows]), "sub", 2, 1, tiled=True
    )
    q_h, k_h, v_h = qkv[0], qkv[1], qkv[2]

    kv = jnp.stack([k_h, v_h])
    pieces = [shifted(kv, "grp", m) for m in range(reach, 0, -1)] + [kv]
    kv_span = jnp.concatenate(pieces, axis=1)
    key_span, value_span = kv_span[0], kv_span[1]

    own_pos = my_grp * blk + jnp.arange(blk, dtype=jnp.int32)
    key_pos = (my_grp - reach) * blk + jnp.arange(span_len, dtype=jnp.int32)
    allowed = in_band(own_pos, key_pos, limit)
    scores = (
        jnp.einsum("rd,kd->rk", q_h, key_span, preferred_element_type=jnp.float32) * scale
    )
    scores = jnp.where(allowed, scores, masked_score)
    row_max = jnp.max(scores, axis=1, keepdims=True)
    log_total = row_max + jnp.log(jnp.sum(jnp.exp(scores - row_max), axis=1, keepdims=True))
    probs = jnp.where(allowed, jnp.exp(scores - log_total), 0.0)
    weights = probs.astype(jnp.bfloat16)
    att_h = jnp.einsum(
        "rk,kd->rd", weights, value_span, preferred_element_type=jnp.float32
    ).astype(jnp.bfloat16)

    far = lax.ppermute(d_out, "tensor", [(t, t ^ 2) for t in range(n_tensor)])
    near = lax.ppermute(
        jnp.stack([d_out, far]), "tensor", [(t, t ^ 1) for t in range(n_tensor)]
    )
    by_xor = jnp.stack([d_out, near[0], far, near[1]])
    order = jnp.arange(n_tensor, dtype=jnp.int32) ^ my_t
    d_out_full = jnp.moveaxis(jnp.take(by_xor, order, axis=0), 0, 1).reshape(tok_rows, -1)
    d_attended = lax.dot_general(
        d_out_full,
        w_out,
        (((1,), (1,)), ((), ())),
        preferred_element_type=jnp.float32,
    ).astype(jnp.bfloat16)
    d_h = lax.all_to_all(d_attended, "sub", 1, 0, tiled=True)
    delta = jnp.sum(d_h.astype(jnp.float32) * att_h.astype(jnp.float32), axis=1)

    d_probs = jnp.einsum("rd,kd->rk", d_h, value_span, preferred_element_type=jnp.float32)
    d_scores = (scale * probs * (d_probs - delta[:, None])).astype(jnp.bfloat16)
    dq_h = jnp.einsum(
        "rk,kd->rd", d_scores, key_span, preferred_element_type=jnp.float32
    ).astype(jnp.bfloat16)
    att_dq = lax.all_to_all(jnp.stack([att_h, dq_h]), "sub", 1, 2, tiled=True)
    attended, d_queries = att_dq[0], att_dq[1]
    partial_out = jnp.dot(attended, w_out, preferred_element_type=jnp.float32)
    my_core = my_t % 2
    my_hi = my_t // 2
    parts = partial_out.astype(jnp.bfloat16).reshape(tok_rows, n_tensor // 2, 2, -1)
    keep = lax.dynamic_index_in_dim(parts, my_core, 2, keepdims=False)
    send = lax.dynamic_index_in_dim(parts, 1 - my_core, 2, keepdims=False)
    got = lax.ppermute(send, "tensor", [(t, t ^ 1) for t in range(n_tensor)])
    chip_sum = keep.astype(jnp.float32) + got.astype(jnp.float32)
    mine = lax.dynamic_index_in_dim(chip_sum, my_hi, 1, keepdims=False)
    other = lax.dynamic_index_in_dim(chip_sum, 1 - my_hi, 1, keepdims=False)
    got2 = lax.ppermute(
        other.astype(jnp.bfloat16), "tensor", [(t, t ^ 2) for t in range(n_tensor)]
    )
    output = (mine + got2.astype(jnp.float32)).astype(jnp.bfloat16)


    pair = jnp.stack([q_h, d_h])
    stats = jnp.stack([log_total[:, 0], delta])
    hi = lax.reduce_precision(stats, exponent_bits=8, mantissa_bits=7)
    rest = stats - hi
    mid = lax.reduce_precision(rest, exponent_bits=8, mantissa_bits=7)
    lo = rest - mid
    split = jnp.concatenate([hi, mid, lo]).astype(jnp.bfloat16)
    n_stat_rows = split.size // HD
    packed = jnp.concatenate(
        [pair.reshape(-1, HD), split.reshape(n_stat_rows, HD)], axis=0
    )
    pair_pieces = [pair]
    stat_pieces = [stats]
    for m in range(1, reach + 1):
        got = shifted(packed, "grp", -m)
        pair_pieces.append(got[: pair.size // HD].reshape(pair.shape))
        parts3 = got[pair.size // HD :].reshape(3, 2, blk).astype(jnp.float32)
        stat_pieces.append((parts3[0] + parts3[1]) + parts3[2])
    pair_span = jnp.concatenate(pair_pieces, axis=1)
    stat_span = jnp.concatenate(stat_pieces, axis=1)
    later_q, later_d = pair_span[0], pair_span[1]
    later_pos = my_grp * blk + jnp.arange(span_len, dtype=jnp.int32)
    allowed_back = in_band(later_pos, own_pos, limit)
    scores_back = (
        jnp.einsum("qd,kd->qk", later_q, k_h, preferred_element_type=jnp.float32) * scale
    )
    probs_back = jnp.where(allowed_back, jnp.exp(scores_back - stat_span[0][:, None]), 0.0)
    d_probs_back = jnp.einsum("qd,kd->qk", later_d, v_h, preferred_element_type=jnp.float32)
    d_scores_back = (scale * probs_back * (d_probs_back - stat_span[1][:, None])).astype(
        jnp.bfloat16
    )
    dk_h = jnp.einsum(
        "qk,qd->kd", d_scores_back, later_q, preferred_element_type=jnp.float32
    ).astype(jnp.bfloat16)
    dv_h = jnp.einsum(
        "qk,qd->kd", probs_back.astype(jnp.bfloat16), later_d, preferred_element_type=jnp.float32
    ).astype(jnp.bfloat16)

    grads = lax.all_to_all(jnp.stack([dk_h, dv_h]), "sub", 1, 2, tiled=True)
    return (output, d_queries, grads[0], grads[1])


def solution(mesh):
    n_seq, n_tensor = mesh.devices.shape
    heads_dev = 2048 // HD // n_tensor
    regrouped = Mesh(
        mesh.devices.reshape(n_seq // heads_dev, heads_dev, n_tensor), ("grp", "sub", "tensor")
    )
    rows = P(("grp", "sub"), "tensor")
    placed = (rows, rows, rows, P("tensor", None), rows)
    return jax.shard_map(
        body,
        mesh=regrouped,
        in_specs=placed,
        out_specs=(rows, rows, rows, rows),
        check_vma=False,
    )
```

```python
import math

import jax
import jax.numpy as jnp
from jax import lax
import functools

from jax.experimental import pallas as pl
from jax.experimental.pallas import tpu as pltpu
from jax.sharding import Mesh
from jax.sharding import PartitionSpec as P

HD = 128
WINDOW = 2048


masked_score = -1e30


def shifted(block, axis, distance):
    devices = range(lax.axis_size(axis))
    route = [(i - distance, i) for i in devices if i - distance in devices]
    return lax.ppermute(block, axis, route)


def in_band(query_pos, key_pos, limit):
    return (
        (key_pos[None, :] <= query_pos[:, None])
        & (key_pos[None, :] > query_pos[:, None] - WINDOW)
        & (key_pos[None, :] >= 0)
        & (query_pos[:, None] < limit)
    )


def _kside_kernel(valid_ref, q_ref, d_ref, lse_ref, dl_ref, k_ref, v_ref, dk_ref, dv_ref, dk_acc, dv_acc, *, scale, qblk):
    i = pl.program_id(0)
    @pl.when(i == 0)
    def _():
        dk_acc[...] = jnp.zeros_like(dk_acc)
        dv_acc[...] = jnp.zeros_like(dv_acc)
    q = q_ref[...]
    d = d_ref[...]
    k = k_ref[...]
    v = v_ref[...]
    s = lax.dot_general(q, k, (((1,), (1,)), ((), ())), preferred_element_type=jnp.float32) * scale
    nk = k.shape[0]
    rq = i * qblk + lax.broadcasted_iota(jnp.int32, (qblk, nk), 0)
    rk = lax.broadcasted_iota(jnp.int32, (qblk, nk), 1)
    ok = (rk <= rq) & (rk > rq - WINDOW) & (rq < valid_ref[0])
    p = jnp.where(ok, jnp.exp(s - lse_ref[...]), 0.0)
    dp = lax.dot_general(d, v, (((1,), (1,)), ((), ())), preferred_element_type=jnp.float32)
    ds = (scale * p * (dp - dl_ref[...])).astype(jnp.bfloat16)
    dk_acc[...] += lax.dot_general(ds, q, (((0,), (0,)), ((), ())), preferred_element_type=jnp.float32)
    dv_acc[...] += lax.dot_general(p.astype(jnp.bfloat16), d, (((0,), (0,)), ((), ())), preferred_element_type=jnp.float32)
    @pl.when(i == pl.num_programs(0) - 1)
    def _():
        dk_ref[...] = dk_acc[...].astype(dk_ref.dtype)
        dv_ref[...] = dv_acc[...].astype(dv_ref.dtype)

def key_side(valid, later_q, later_d, lse, delta, k_h, v_h, qblk=512):
    span, hd = later_q.shape
    nk = k_h.shape[0]
    scale = 1.0 / math.sqrt(HD)
    kern = functools.partial(_kside_kernel, scale=scale, qblk=qblk)
    return pl.pallas_call(
        kern,
        grid=(span // qblk,),
        in_specs=[
            pl.BlockSpec(memory_space=pltpu.SMEM),
            pl.BlockSpec((qblk, hd), lambda i: (i, 0)),
            pl.BlockSpec((qblk, hd), lambda i: (i, 0)),
            pl.BlockSpec((qblk, 1), lambda i: (i, 0)),
            pl.BlockSpec((qblk, 1), lambda i: (i, 0)),
            pl.BlockSpec((nk, hd), lambda i: (0, 0)),
            pl.BlockSpec((nk, hd), lambda i: (0, 0)),
        ],
        out_specs=[pl.BlockSpec((nk, hd), lambda i: (0, 0)), pl.BlockSpec((nk, hd), lambda i: (0, 0))],
        out_shape=[jax.ShapeDtypeStruct((nk, hd), jnp.bfloat16)] * 2,
        scratch_shapes=[pltpu.VMEM((nk, hd), jnp.float32), pltpu.VMEM((nk, hd), jnp.float32)],
        compiler_params=pltpu.CompilerParams(dimension_semantics=("arbitrary",)),
    )(valid, later_q, later_d, lse.reshape(span, 1), delta.reshape(span, 1), k_h, v_h)


def body(query_rows, key_rows, value_rows, w_out, d_out):
    tok_rows, col_dev = query_rows.shape
    n_grp = lax.axis_size("grp")
    n_sub = lax.axis_size("sub")
    my_grp = lax.axis_index("grp")
    blk = tok_rows * n_sub
    reach = min(-(-WINDOW // blk), n_grp - 1)
    span_len = (reach + 1) * blk
    scale = 1.0 / math.sqrt(HD)
    limit = blk * n_grp
    n_tensor = lax.axis_size("tensor")
    my_t = lax.axis_index("tensor")

    qkv = lax.all_to_all(
        jnp.stack([query_rows, key_rows, value_rows]), "sub", 2, 1, tiled=True
    )
    q_h, k_h, v_h = qkv[0], qkv[1], qkv[2]

    kv = jnp.stack([k_h, v_h])
    pieces = [shifted(kv, "grp", m) for m in range(reach, 0, -1)] + [kv]
    kv_span = jnp.concatenate(pieces, axis=1)
    key_span, value_span = kv_span[0], kv_span[1]

    own_pos = my_grp * blk + jnp.arange(blk, dtype=jnp.int32)
    key_pos = (my_grp - reach) * blk + jnp.arange(span_len, dtype=jnp.int32)
    allowed = in_band(own_pos, key_pos, limit)
    scores = (
        jnp.einsum("rd,kd->rk", q_h, key_span, preferred_element_type=jnp.float32) * scale
    )
    scores = jnp.where(allowed, scores, masked_score)
    row_max = jnp.max(scores, axis=1, keepdims=True)
    log_total = row_max + jnp.log(jnp.sum(jnp.exp(scores - row_max), axis=1, keepdims=True))
    probs = jnp.where(allowed, jnp.exp(scores - log_total), 0.0)
    weights = probs.astype(jnp.bfloat16)
    att_h = jnp.einsum(
        "rk,kd->rd", weights, value_span, preferred_element_type=jnp.float32
    ).astype(jnp.bfloat16)

    far = lax.ppermute(d_out, "tensor", [(t, t ^ 2) for t in range(n_tensor)])
    near = lax.ppermute(
        jnp.stack([d_out, far]), "tensor", [(t, t ^ 1) for t in range(n_tensor)]
    )
    by_xor = jnp.stack([d_out, near[0], far, near[1]])
    order = jnp.arange(n_tensor, dtype=jnp.int32) ^ my_t
    d_out_full = jnp.moveaxis(jnp.take(by_xor, order, axis=0), 0, 1).reshape(tok_rows, -1)
    d_attended = lax.dot_general(
        d_out_full,
        w_out,
        (((1,), (1,)), ((), ())),
        preferred_element_type=jnp.float32,
    ).astype(jnp.bfloat16)
    d_h = lax.all_to_all(d_attended, "sub", 1, 0, tiled=True)
    delta = jnp.sum(d_h.astype(jnp.float32) * att_h.astype(jnp.float32), axis=1)

    d_probs = jnp.einsum("rd,kd->rk", d_h, value_span, preferred_element_type=jnp.float32)
    d_scores = (scale * probs * (d_probs - delta[:, None])).astype(jnp.bfloat16)
    dq_h = jnp.einsum(
        "rk,kd->rd", d_scores, key_span, preferred_element_type=jnp.float32
    ).astype(jnp.bfloat16)
    att_dq = lax.all_to_all(jnp.stack([att_h, dq_h]), "sub", 1, 2, tiled=True)
    attended, d_queries = att_dq[0], att_dq[1]
    partial_out = jnp.dot(attended, w_out, preferred_element_type=jnp.float32)
    my_core = my_t % 2
    my_hi = my_t // 2
    parts = partial_out.astype(jnp.bfloat16).reshape(tok_rows, n_tensor // 2, 2, -1)
    keep = lax.dynamic_index_in_dim(parts, my_core, 2, keepdims=False)
    send = lax.dynamic_index_in_dim(parts, 1 - my_core, 2, keepdims=False)
    got = lax.ppermute(send, "tensor", [(t, t ^ 1) for t in range(n_tensor)])
    chip_sum = keep.astype(jnp.float32) + got.astype(jnp.float32)
    mine = lax.dynamic_index_in_dim(chip_sum, my_hi, 1, keepdims=False)
    other = lax.dynamic_index_in_dim(chip_sum, 1 - my_hi, 1, keepdims=False)
    got2 = lax.ppermute(
        other.astype(jnp.bfloat16), "tensor", [(t, t ^ 2) for t in range(n_tensor)]
    )
    output = (mine + got2.astype(jnp.float32)).astype(jnp.bfloat16)


    pair = jnp.stack([q_h, d_h])
    stats = jnp.stack([log_total[:, 0], delta])
    hi = lax.reduce_precision(stats, exponent_bits=8, mantissa_bits=7)
    rest = stats - hi
    mid = lax.reduce_precision(rest, exponent_bits=8, mantissa_bits=7)
    lo = rest - mid
    split = jnp.concatenate([hi, mid, lo]).astype(jnp.bfloat16)
    n_stat_rows = split.size // HD
    packed = jnp.concatenate(
        [pair.reshape(-1, HD), split.reshape(n_stat_rows, HD)], axis=0
    )
    pair_pieces = [pair]
    stat_pieces = [stats]
    for m in range(1, reach + 1):
        got = shifted(packed, "grp", -m)
        pair_pieces.append(got[: pair.size // HD].reshape(pair.shape))
        parts3 = got[pair.size // HD :].reshape(3, 2, blk).astype(jnp.float32)
        stat_pieces.append((parts3[0] + parts3[1]) + parts3[2])
    pair_span = jnp.concatenate(pair_pieces, axis=1)
    stat_span = jnp.concatenate(stat_pieces, axis=1)
    later_q, later_d = pair_span[0], pair_span[1]
    valid = jnp.reshape(limit - my_grp * blk, (1,)).astype(jnp.int32)
    dk_h, dv_h = key_side(
        valid, later_q, later_d, stat_span[0], stat_span[1], k_h, v_h, qblk=blk
    )

    grads = lax.all_to_all(jnp.stack([dk_h, dv_h]), "sub", 1, 2, tiled=True)
    return (output, d_queries, grads[0], grads[1])


def solution(mesh):
    n_seq, n_tensor = mesh.devices.shape
    heads_dev = 2048 // HD // n_tensor
    regrouped = Mesh(
        mesh.devices.reshape(n_seq // heads_dev, heads_dev, n_tensor), ("grp", "sub", "tensor")
    )
    rows = P(("grp", "sub"), "tensor")
    placed = (rows, rows, rows, P("tensor", None), rows)
    return jax.shard_map(
        body,
        mesh=regrouped,
        in_specs=placed,
        out_specs=(rows, rows, rows, rows),
        check_vma=False,
    )
```

```python
import math

import jax
import jax.numpy as jnp
from jax import lax
import functools

from jax.experimental import pallas as pl
from jax.experimental.pallas import tpu as pltpu
from jax.sharding import Mesh
from jax.sharding import PartitionSpec as P

HD = 128
WINDOW = 2048


masked_score = -1e30


def shifted(block, axis, distance):
    devices = range(lax.axis_size(axis))
    route = [(i - distance, i) for i in devices if i - distance in devices]
    return lax.ppermute(block, axis, route)


def in_band(query_pos, key_pos, limit):
    return (
        (key_pos[None, :] <= query_pos[:, None])
        & (key_pos[None, :] > query_pos[:, None] - WINDOW)
        & (key_pos[None, :] >= 0)
        & (query_pos[:, None] < limit)
    )


def _kside_kernel(off_ref, q_ref, d_ref, st_ref, k_ref, v_ref, dk0_ref, dv0_ref, dk_ref, dv_ref, dk_acc, dv_acc, *, scale, qblk):
    i = pl.program_id(0)
    @pl.when(i == 0)
    def _():
        dk_acc[...] = dk0_ref[...]
        dv_acc[...] = dv0_ref[...]
    q = q_ref[...]
    d = d_ref[...]
    k = k_ref[...]
    v = v_ref[...]
    nk = k.shape[0]
    st = lax.dot_general(k, q, (((1,), (1,)), ((), ())), preferred_element_type=jnp.float32) * scale
    rk = lax.broadcasted_iota(jnp.int32, (nk, qblk), 0)
    rq = off_ref[0] + i * qblk + lax.broadcasted_iota(jnp.int32, (nk, qblk), 1)
    ok = (rk <= rq) & (rk > rq - WINDOW) & (rq < off_ref[1])
    stats = st_ref[...]
    p = jnp.where(ok, jnp.exp(st - stats[0:1, :]), 0.0)
    dp = lax.dot_general(v, d, (((1,), (1,)), ((), ())), preferred_element_type=jnp.float32)
    ds = (scale * p * (dp - stats[1:2, :])).astype(jnp.bfloat16)
    dk_acc[...] += jnp.dot(ds, q, preferred_element_type=jnp.float32)
    dv_acc[...] += jnp.dot(p.astype(jnp.bfloat16), d, preferred_element_type=jnp.float32)
    @pl.when(i == pl.num_programs(0) - 1)
    def _():
        dk_ref[...] = dk_acc[...].astype(dk_ref.dtype)
        dv_ref[...] = dv_acc[...].astype(dv_ref.dtype)

def key_side(off, later_q, later_d, stats, k_h, v_h, dk0, dv0, out_dtype, qblk=512):
    span, hd = later_q.shape
    nk = k_h.shape[0]
    scale = 1.0 / math.sqrt(HD)
    kern = functools.partial(_kside_kernel, scale=scale, qblk=qblk)
    return pl.pallas_call(
        kern,
        grid=(span // qblk,),
        in_specs=[
            pl.BlockSpec(memory_space=pltpu.SMEM),
            pl.BlockSpec((qblk, hd), lambda i: (i, 0)),
            pl.BlockSpec((qblk, hd), lambda i: (i, 0)),
            pl.BlockSpec((2, qblk), lambda i: (0, i)),
            pl.BlockSpec((nk, hd), lambda i: (0, 0)),
            pl.BlockSpec((nk, hd), lambda i: (0, 0)),
            pl.BlockSpec((nk, hd), lambda i: (0, 0)),
            pl.BlockSpec((nk, hd), lambda i: (0, 0)),
        ],
        out_specs=[pl.BlockSpec((nk, hd), lambda i: (0, 0)), pl.BlockSpec((nk, hd), lambda i: (0, 0))],
        out_shape=[jax.ShapeDtypeStruct((nk, hd), out_dtype)] * 2,
        scratch_shapes=[pltpu.VMEM((nk, hd), jnp.float32), pltpu.VMEM((nk, hd), jnp.float32)],
        compiler_params=pltpu.CompilerParams(dimension_semantics=("arbitrary",)),
    )(off, later_q, later_d, stats, k_h, v_h, dk0, dv0)


def body(query_rows, key_rows, value_rows, w_out, d_out):
    tok_rows, col_dev = query_rows.shape
    n_grp = lax.axis_size("grp")
    n_sub = lax.axis_size("sub")
    my_grp = lax.axis_index("grp")
    blk = tok_rows * n_sub
    reach = min(-(-WINDOW // blk), n_grp - 1)
    span_len = (reach + 1) * blk
    scale = 1.0 / math.sqrt(HD)
    limit = blk * n_grp
    n_tensor = lax.axis_size("tensor")
    my_t = lax.axis_index("tensor")

    qkv = lax.all_to_all(
        jnp.stack([query_rows, key_rows, value_rows]), "sub", 2, 1, tiled=True
    )
    q_h, k_h, v_h = qkv[0], qkv[1], qkv[2]

    kv = jnp.stack([k_h, v_h])
    pieces = [shifted(kv, "grp", m) for m in range(reach, 0, -1)] + [kv]
    kv_span = jnp.concatenate(pieces, axis=1)
    key_span, value_span = kv_span[0], kv_span[1]

    own_pos = my_grp * blk + jnp.arange(blk, dtype=jnp.int32)
    key_pos = (my_grp - reach) * blk + jnp.arange(span_len, dtype=jnp.int32)
    allowed = in_band(own_pos, key_pos, limit)
    scores = (
        jnp.einsum("rd,kd->rk", q_h, key_span, preferred_element_type=jnp.float32) * scale
    )
    scores = jnp.where(allowed, scores, masked_score)
    row_max = jnp.max(scores, axis=1, keepdims=True)
    log_total = row_max + jnp.log(jnp.sum(jnp.exp(scores - row_max), axis=1, keepdims=True))
    probs = jnp.where(allowed, jnp.exp(scores - log_total), 0.0)
    weights = probs.astype(jnp.bfloat16)
    att_h = jnp.einsum(
        "rk,kd->rd", weights, value_span, preferred_element_type=jnp.float32
    ).astype(jnp.bfloat16)

    far = lax.ppermute(d_out, "tensor", [(t, t ^ 2) for t in range(n_tensor)])
    near = lax.ppermute(
        jnp.stack([d_out, far]), "tensor", [(t, t ^ 1) for t in range(n_tensor)]
    )
    by_xor = jnp.stack([d_out, near[0], far, near[1]])
    order = jnp.arange(n_tensor, dtype=jnp.int32) ^ my_t
    d_out_full = jnp.moveaxis(jnp.take(by_xor, order, axis=0), 0, 1).reshape(tok_rows, -1)
    d_attended = lax.dot_general(
        d_out_full,
        w_out,
        (((1,), (1,)), ((), ())),
        preferred_element_type=jnp.float32,
    ).astype(jnp.bfloat16)
    d_h = lax.all_to_all(d_attended, "sub", 1, 0, tiled=True)
    delta = jnp.sum(d_h.astype(jnp.float32) * att_h.astype(jnp.float32), axis=1)

    d_probs = jnp.einsum("rd,kd->rk", d_h, value_span, preferred_element_type=jnp.float32)
    d_scores = (scale * probs * (d_probs - delta[:, None])).astype(jnp.bfloat16)
    dq_h = jnp.einsum(
        "rk,kd->rd", d_scores, key_span, preferred_element_type=jnp.float32
    ).astype(jnp.bfloat16)
    att_dq = lax.all_to_all(jnp.stack([att_h, dq_h]), "sub", 1, 2, tiled=True)
    attended, d_queries = att_dq[0], att_dq[1]
    partial_out = jnp.dot(attended, w_out, preferred_element_type=jnp.float32)
    my_core = my_t % 2
    my_hi = my_t // 2
    parts = partial_out.astype(jnp.bfloat16).reshape(tok_rows, n_tensor // 2, 2, -1)
    keep = lax.dynamic_index_in_dim(parts, my_core, 2, keepdims=False)
    send = lax.dynamic_index_in_dim(parts, 1 - my_core, 2, keepdims=False)
    got = lax.ppermute(send, "tensor", [(t, t ^ 1) for t in range(n_tensor)])
    chip_sum = keep.astype(jnp.float32) + got.astype(jnp.float32)
    mine = lax.dynamic_index_in_dim(chip_sum, my_hi, 1, keepdims=False)
    other = lax.dynamic_index_in_dim(chip_sum, 1 - my_hi, 1, keepdims=False)
    got2 = lax.ppermute(
        other.astype(jnp.bfloat16), "tensor", [(t, t ^ 2) for t in range(n_tensor)]
    )
    output = (mine + got2.astype(jnp.float32)).astype(jnp.bfloat16)


    pair = jnp.stack([q_h, d_h])
    stats = jnp.stack([log_total[:, 0], delta])
    hi = lax.reduce_precision(stats, exponent_bits=8, mantissa_bits=7)
    rest = stats - hi
    mid = lax.reduce_precision(rest, exponent_bits=8, mantissa_bits=7)
    lo = rest - mid
    split = jnp.concatenate([hi, mid, lo]).astype(jnp.bfloat16)
    n_stat_rows = split.size // HD
    packed = jnp.concatenate(
        [pair.reshape(-1, HD), split.reshape(n_stat_rows, HD)], axis=0
    )
    pair_pieces = [pair]
    stat_pieces = [stats]
    for m in range(1, reach + 1):
        got = shifted(packed, "grp", -m)
        pair_pieces.append(got[: pair.size // HD].reshape(pair.shape))
        parts3 = got[pair.size // HD :].reshape(3, 2, blk).astype(jnp.float32)
        stat_pieces.append((parts3[0] + parts3[1]) + parts3[2])
    valid = limit - my_grp * blk
    acc0 = jnp.zeros((blk, HD), jnp.float32)
    dk_own, dv_own = key_side(
        jnp.stack([0, valid]).astype(jnp.int32), q_h, d_h, stats, k_h, v_h,
        acc0, acc0, jnp.float32, qblk=blk,
    )
    later = jnp.concatenate(pair_pieces[1:], axis=1)
    later_stats = jnp.concatenate(stat_pieces[1:], axis=1)
    dk_h, dv_h = key_side(
        jnp.stack([blk, valid]).astype(jnp.int32), later[0], later[1], later_stats, k_h, v_h,
        dk_own, dv_own, jnp.bfloat16, qblk=blk,
    )

    grads = lax.all_to_all(jnp.stack([dk_h, dv_h]), "sub", 1, 2, tiled=True)
    return (output, d_queries, grads[0], grads[1])


def solution(mesh):
    n_seq, n_tensor = mesh.devices.shape
    heads_dev = 2048 // HD // n_tensor
    regrouped = Mesh(
        mesh.devices.reshape(n_seq // heads_dev, heads_dev, n_tensor), ("grp", "sub", "tensor")
    )
    rows = P(("grp", "sub"), "tensor")
    placed = (rows, rows, rows, P("tensor", None), rows)
    return jax.shard_map(
        body,
        mesh=regrouped,
        in_specs=placed,
        out_specs=(rows, rows, rows, rows),
        check_vma=False,
    )
```

```python
import math

import jax
import jax.numpy as jnp
from jax import lax
import functools

from jax.experimental import pallas as pl
from jax.experimental.pallas import tpu as pltpu
from jax.sharding import Mesh
from jax.sharding import PartitionSpec as P

HD = 128
WINDOW = 2048


masked_score = -1e30


def shifted(block, axis, distance):
    devices = range(lax.axis_size(axis))
    route = [(i - distance, i) for i in devices if i - distance in devices]
    return lax.ppermute(block, axis, route)


def in_band(query_pos, key_pos, limit):
    return (
        (key_pos[None, :] <= query_pos[:, None])
        & (key_pos[None, :] > query_pos[:, None] - WINDOW)
        & (key_pos[None, :] >= 0)
        & (query_pos[:, None] < limit)
    )


def _kside_kernel(off_ref, q_ref, d_ref, st_ref, k_ref, v_ref, dk0_ref, dv0_ref, dk_ref, dv_ref, dk_acc, dv_acc, *, scale, qblk):
    i = pl.program_id(0)
    @pl.when(i == 0)
    def _():
        dk_acc[...] = dk0_ref[...]
        dv_acc[...] = dv0_ref[...]
    q = q_ref[...]
    d = d_ref[...]
    k = k_ref[...]
    v = v_ref[...]
    nk = k.shape[0]
    st = lax.dot_general(k, q, (((1,), (1,)), ((), ())), preferred_element_type=jnp.float32) * scale
    rk = lax.broadcasted_iota(jnp.int32, (nk, qblk), 0)
    rq = off_ref[0] + i * qblk + lax.broadcasted_iota(jnp.int32, (nk, qblk), 1)
    ok = (rk <= rq) & (rk > rq - WINDOW) & (rq < off_ref[1])
    stats = st_ref[...]
    p = jnp.where(ok, jnp.exp(st - stats[0:1, :]), 0.0)
    dp = lax.dot_general(v, d, (((1,), (1,)), ((), ())), preferred_element_type=jnp.float32)
    ds = (scale * p * (dp - stats[1:2, :])).astype(jnp.bfloat16)
    dk_acc[...] += jnp.dot(ds, q, preferred_element_type=jnp.float32)
    dv_acc[...] += jnp.dot(p.astype(jnp.bfloat16), d, preferred_element_type=jnp.float32)
    @pl.when(i == pl.num_programs(0) - 1)
    def _():
        dk_ref[...] = dk_acc[...].astype(dk_ref.dtype)
        dv_ref[...] = dv_acc[...].astype(dv_ref.dtype)

def key_side(off, later_q, later_d, stats, k_h, v_h, dk0, dv0, out_dtype, qblk=512):
    span, hd = later_q.shape
    nk = k_h.shape[0]
    scale = 1.0 / math.sqrt(HD)
    kern = functools.partial(_kside_kernel, scale=scale, qblk=qblk)
    return pl.pallas_call(
        kern,
        grid=(span // qblk,),
        in_specs=[
            pl.BlockSpec(memory_space=pltpu.SMEM),
            pl.BlockSpec((qblk, hd), lambda i: (i, 0)),
            pl.BlockSpec((qblk, hd), lambda i: (i, 0)),
            pl.BlockSpec((2, qblk), lambda i: (0, i)),
            pl.BlockSpec((nk, hd), lambda i: (0, 0)),
            pl.BlockSpec((nk, hd), lambda i: (0, 0)),
            pl.BlockSpec((nk, hd), lambda i: (0, 0)),
            pl.BlockSpec((nk, hd), lambda i: (0, 0)),
        ],
        out_specs=[pl.BlockSpec((nk, hd), lambda i: (0, 0)), pl.BlockSpec((nk, hd), lambda i: (0, 0))],
        out_shape=[jax.ShapeDtypeStruct((nk, hd), out_dtype)] * 2,
        scratch_shapes=[pltpu.VMEM((nk, hd), jnp.float32), pltpu.VMEM((nk, hd), jnp.float32)],
        compiler_params=pltpu.CompilerParams(dimension_semantics=("arbitrary",)),
    )(off, later_q, later_d, stats, k_h, v_h, dk0, dv0)


def body(query_rows, key_rows, value_rows, w_out, d_out):
    tok_rows, col_dev = query_rows.shape
    n_grp = lax.axis_size("grp")
    n_sub = lax.axis_size("sub")
    my_grp = lax.axis_index("grp")
    blk = tok_rows * n_sub
    reach = min(-(-WINDOW // blk), n_grp - 1)
    span_len = (reach + 1) * blk
    scale = 1.0 / math.sqrt(HD)
    limit = blk * n_grp
    n_tensor = lax.axis_size("tensor")
    my_t = lax.axis_index("tensor")

    qkv = lax.all_to_all(
        jnp.stack([query_rows, key_rows, value_rows]), "sub", 2, 1, tiled=True
    )
    q_h, k_h, v_h = qkv[0], qkv[1], qkv[2]

    kv = jnp.stack([k_h, v_h])
    pieces = [shifted(kv, "grp", m) for m in range(reach, 0, -1)] + [kv]
    kv_span = jnp.concatenate(pieces, axis=1)
    d_out, kv_span = lax.optimization_barrier((d_out, kv_span))
    key_span, value_span = kv_span[0], kv_span[1]

    own_pos = my_grp * blk + jnp.arange(blk, dtype=jnp.int32)
    key_pos = (my_grp - reach) * blk + jnp.arange(span_len, dtype=jnp.int32)
    allowed = in_band(own_pos, key_pos, limit)
    scores = (
        jnp.einsum("rd,kd->rk", q_h, key_span, preferred_element_type=jnp.float32) * scale
    )
    scores = jnp.where(allowed, scores, masked_score)
    row_max = jnp.max(scores, axis=1, keepdims=True)
    log_total = row_max + jnp.log(jnp.sum(jnp.exp(scores - row_max), axis=1, keepdims=True))
    probs = jnp.where(allowed, jnp.exp(scores - log_total), 0.0)
    weights = probs.astype(jnp.bfloat16)
    att_h = jnp.einsum(
        "rk,kd->rd", weights, value_span, preferred_element_type=jnp.float32
    ).astype(jnp.bfloat16)

    far = lax.ppermute(d_out, "tensor", [(t, t ^ 2) for t in range(n_tensor)])
    near = lax.ppermute(
        jnp.stack([d_out, far]), "tensor", [(t, t ^ 1) for t in range(n_tensor)]
    )
    by_xor = jnp.stack([d_out, near[0], far, near[1]])
    order = jnp.arange(n_tensor, dtype=jnp.int32) ^ my_t
    d_out_full = jnp.moveaxis(jnp.take(by_xor, order, axis=0), 0, 1).reshape(tok_rows, -1)
    d_attended = lax.dot_general(
        d_out_full,
        w_out,
        (((1,), (1,)), ((), ())),
        preferred_element_type=jnp.float32,
    ).astype(jnp.bfloat16)
    d_h = lax.all_to_all(d_attended, "sub", 1, 0, tiled=True)
    delta = jnp.sum(d_h.astype(jnp.float32) * att_h.astype(jnp.float32), axis=1)

    d_probs = jnp.einsum("rd,kd->rk", d_h, value_span, preferred_element_type=jnp.float32)
    d_scores = (scale * probs * (d_probs - delta[:, None])).astype(jnp.bfloat16)
    dq_h = jnp.einsum(
        "rk,kd->rd", d_scores, key_span, preferred_element_type=jnp.float32
    ).astype(jnp.bfloat16)
    att_dq = lax.all_to_all(jnp.stack([att_h, dq_h]), "sub", 1, 2, tiled=True)
    attended, d_queries = att_dq[0], att_dq[1]
    partial_out = jnp.dot(attended, w_out, preferred_element_type=jnp.float32)
    my_core = my_t % 2
    my_hi = my_t // 2
    parts = partial_out.astype(jnp.bfloat16).reshape(tok_rows, n_tensor // 2, 2, -1)
    keep = lax.dynamic_index_in_dim(parts, my_core, 2, keepdims=False)
    send = lax.dynamic_index_in_dim(parts, 1 - my_core, 2, keepdims=False)
    got = lax.ppermute(send, "tensor", [(t, t ^ 1) for t in range(n_tensor)])
    chip_sum = keep.astype(jnp.float32) + got.astype(jnp.float32)
    mine = lax.dynamic_index_in_dim(chip_sum, my_hi, 1, keepdims=False)
    other = lax.dynamic_index_in_dim(chip_sum, 1 - my_hi, 1, keepdims=False)
    got2 = lax.ppermute(
        other.astype(jnp.bfloat16), "tensor", [(t, t ^ 2) for t in range(n_tensor)]
    )
    output = (mine + got2.astype(jnp.float32)).astype(jnp.bfloat16)


    pair = jnp.stack([q_h, d_h])
    stats = jnp.stack([log_total[:, 0], delta])
    hi = lax.reduce_precision(stats, exponent_bits=8, mantissa_bits=7)
    rest = stats - hi
    mid = lax.reduce_precision(rest, exponent_bits=8, mantissa_bits=7)
    lo = rest - mid
    split = jnp.concatenate([hi, mid, lo]).astype(jnp.bfloat16)
    n_stat_rows = split.size // HD
    packed = jnp.concatenate(
        [pair.reshape(-1, HD), split.reshape(n_stat_rows, HD)], axis=0
    )
    pair_pieces = [pair]
    stat_pieces = [stats]
    for m in range(1, reach + 1):
        got = shifted(packed, "grp", -m)
        pair_pieces.append(got[: pair.size // HD].reshape(pair.shape))
        parts3 = got[pair.size // HD :].reshape(3, 2, blk).astype(jnp.float32)
        stat_pieces.append((parts3[0] + parts3[1]) + parts3[2])
    valid = limit - my_grp * blk
    acc0 = jnp.zeros((blk, HD), jnp.float32)
    dk_own, dv_own = key_side(
        jnp.stack([0, valid]).astype(jnp.int32), q_h, d_h, stats, k_h, v_h,
        acc0, acc0, jnp.float32, qblk=blk,
    )
    later = jnp.concatenate(pair_pieces[1:], axis=1)
    later_stats = jnp.concatenate(stat_pieces[1:], axis=1)
    dk_h, dv_h = key_side(
        jnp.stack([blk, valid]).astype(jnp.int32), later[0], later[1], later_stats, k_h, v_h,
        dk_own, dv_own, jnp.bfloat16, qblk=blk,
    )

    grads = lax.all_to_all(jnp.stack([dk_h, dv_h]), "sub", 1, 2, tiled=True)
    return (output, d_queries, grads[0], grads[1])


def solution(mesh):
    n_seq, n_tensor = mesh.devices.shape
    heads_dev = 2048 // HD // n_tensor
    regrouped = Mesh(
        mesh.devices.reshape(n_seq // heads_dev, heads_dev, n_tensor), ("grp", "sub", "tensor")
    )
    rows = P(("grp", "sub"), "tensor")
    placed = (rows, rows, rows, P("tensor", None), rows)
    return jax.shard_map(
        body,
        mesh=regrouped,
        in_specs=placed,
        out_specs=(rows, rows, rows, rows),
        check_vma=False,
    )
```

```python
import math

import jax
import jax.numpy as jnp
from jax import lax
import functools

from jax.experimental import pallas as pl
from jax.experimental.pallas import tpu as pltpu
from jax.sharding import Mesh
from jax.sharding import PartitionSpec as P

HD = 128
WINDOW = 2048


masked_score = -1e30


def shifted(block, axis, distance):
    devices = range(lax.axis_size(axis))
    route = [(i - distance, i) for i in devices if i - distance in devices]
    return lax.ppermute(block, axis, route)


def in_band(query_pos, key_pos, limit):
    return (
        (key_pos[None, :] <= query_pos[:, None])
        & (key_pos[None, :] > query_pos[:, None] - WINDOW)
        & (key_pos[None, :] >= 0)
        & (query_pos[:, None] < limit)
    )


def _kside_kernel(off_ref, q_ref, d_ref, st_ref, k_ref, v_ref, dk0_ref, dv0_ref, dk_ref, dv_ref, dk_acc, dv_acc, *, scale, qblk):
    i = pl.program_id(0)
    @pl.when(i == 0)
    def _():
        dk_acc[...] = dk0_ref[...]
        dv_acc[...] = dv0_ref[...]
    q = q_ref[...]
    d = d_ref[...]
    k = k_ref[...]
    v = v_ref[...]
    nk = k.shape[0]
    st = lax.dot_general(k, q, (((1,), (1,)), ((), ())), preferred_element_type=jnp.float32) * scale
    rk = lax.broadcasted_iota(jnp.int32, (nk, qblk), 0)
    rq = off_ref[0] + i * qblk + lax.broadcasted_iota(jnp.int32, (nk, qblk), 1)
    ok = (rk <= rq) & (rk > rq - WINDOW) & (rq < off_ref[1])
    stats = st_ref[...]
    p = jnp.where(ok, jnp.exp(st - stats[0:1, :]), 0.0)
    dp = lax.dot_general(v, d, (((1,), (1,)), ((), ())), preferred_element_type=jnp.float32)
    ds = (scale * p * (dp - stats[1:2, :])).astype(jnp.bfloat16)
    dk_acc[...] += jnp.dot(ds, q, preferred_element_type=jnp.float32)
    dv_acc[...] += jnp.dot(p.astype(jnp.bfloat16), d, preferred_element_type=jnp.float32)
    @pl.when(i == pl.num_programs(0) - 1)
    def _():
        dk_ref[...] = dk_acc[...].astype(dk_ref.dtype)
        dv_ref[...] = dv_acc[...].astype(dv_ref.dtype)

def key_side(off, later_q, later_d, stats, k_h, v_h, dk0, dv0, out_dtype, qblk=512):
    span, hd = later_q.shape
    nk = k_h.shape[0]
    scale = 1.0 / math.sqrt(HD)
    kern = functools.partial(_kside_kernel, scale=scale, qblk=qblk)
    return pl.pallas_call(
        kern,
        grid=(span // qblk,),
        in_specs=[
            pl.BlockSpec(memory_space=pltpu.SMEM),
            pl.BlockSpec((qblk, hd), lambda i: (i, 0)),
            pl.BlockSpec((qblk, hd), lambda i: (i, 0)),
            pl.BlockSpec((2, qblk), lambda i: (0, i)),
            pl.BlockSpec((nk, hd), lambda i: (0, 0)),
            pl.BlockSpec((nk, hd), lambda i: (0, 0)),
            pl.BlockSpec((nk, hd), lambda i: (0, 0)),
            pl.BlockSpec((nk, hd), lambda i: (0, 0)),
        ],
        out_specs=[pl.BlockSpec((nk, hd), lambda i: (0, 0)), pl.BlockSpec((nk, hd), lambda i: (0, 0))],
        out_shape=[jax.ShapeDtypeStruct((nk, hd), out_dtype)] * 2,
        scratch_shapes=[pltpu.VMEM((nk, hd), jnp.float32), pltpu.VMEM((nk, hd), jnp.float32)],
        compiler_params=pltpu.CompilerParams(dimension_semantics=("arbitrary",)),
    )(off, later_q, later_d, stats, k_h, v_h, dk0, dv0)


def body(query_rows, key_rows, value_rows, w_out, d_out):
    tok_rows, col_dev = query_rows.shape
    n_grp = lax.axis_size("grp")
    n_sub = lax.axis_size("sub")
    my_grp = lax.axis_index("grp")
    blk = tok_rows * n_sub
    reach = min(-(-WINDOW // blk), n_grp - 1)
    span_len = (reach + 1) * blk
    scale = 1.0 / math.sqrt(HD)
    limit = blk * n_grp
    n_tensor = lax.axis_size("tensor")
    my_t = lax.axis_index("tensor")

    qkv = lax.all_to_all(
        jnp.stack([query_rows, key_rows, value_rows]), "sub", 2, 1, tiled=True
    )
    q_h, k_h, v_h = qkv[0], qkv[1], qkv[2]

    kv = jnp.stack([k_h, v_h])
    pieces = [shifted(kv, "grp", m) for m in range(reach, 0, -1)] + [kv]
    kv_span = jnp.concatenate(pieces, axis=1)
    key_span, value_span = kv_span[0], kv_span[1]

    own_pos = my_grp * blk + jnp.arange(blk, dtype=jnp.int32)
    key_pos = (my_grp - reach) * blk + jnp.arange(span_len, dtype=jnp.int32)
    allowed = in_band(own_pos, key_pos, limit)
    scores = (
        jnp.einsum("rd,kd->rk", q_h, key_span, preferred_element_type=jnp.float32) * scale
    )
    scores = jnp.where(allowed, scores, masked_score)
    row_max = jnp.max(scores, axis=1, keepdims=True)
    log_total = row_max + jnp.log(jnp.sum(jnp.exp(scores - row_max), axis=1, keepdims=True))
    probs = jnp.where(allowed, jnp.exp(scores - log_total), 0.0)
    weights = probs.astype(jnp.bfloat16)
    att_h = jnp.einsum(
        "rk,kd->rd", weights, value_span, preferred_element_type=jnp.float32
    ).astype(jnp.bfloat16)

    far = lax.ppermute(d_out, "tensor", [(t, t ^ 2) for t in range(n_tensor)])
    far, key_span = lax.optimization_barrier((far, key_span))
    near = lax.ppermute(
        jnp.stack([d_out, far]), "tensor", [(t, t ^ 1) for t in range(n_tensor)]
    )
    by_xor = jnp.stack([d_out, near[0], far, near[1]])
    order = jnp.arange(n_tensor, dtype=jnp.int32) ^ my_t
    d_out_full = jnp.moveaxis(jnp.take(by_xor, order, axis=0), 0, 1).reshape(tok_rows, -1)
    d_attended = lax.dot_general(
        d_out_full,
        w_out,
        (((1,), (1,)), ((), ())),
        preferred_element_type=jnp.float32,
    ).astype(jnp.bfloat16)
    d_h = lax.all_to_all(d_attended, "sub", 1, 0, tiled=True)
    delta = jnp.sum(d_h.astype(jnp.float32) * att_h.astype(jnp.float32), axis=1)

    d_probs = jnp.einsum("rd,kd->rk", d_h, value_span, preferred_element_type=jnp.float32)
    d_scores = (scale * probs * (d_probs - delta[:, None])).astype(jnp.bfloat16)
    dq_h = jnp.einsum(
        "rk,kd->rd", d_scores, key_span, preferred_element_type=jnp.float32
    ).astype(jnp.bfloat16)
    att_dq = lax.all_to_all(jnp.stack([att_h, dq_h]), "sub", 1, 2, tiled=True)
    attended, d_queries = att_dq[0], att_dq[1]
    partial_out = jnp.dot(attended, w_out, preferred_element_type=jnp.float32)
    my_core = my_t % 2
    my_hi = my_t // 2
    parts = partial_out.astype(jnp.bfloat16).reshape(tok_rows, n_tensor // 2, 2, -1)
    keep = lax.dynamic_index_in_dim(parts, my_core, 2, keepdims=False)
    send = lax.dynamic_index_in_dim(parts, 1 - my_core, 2, keepdims=False)
    got = lax.ppermute(send, "tensor", [(t, t ^ 1) for t in range(n_tensor)])
    chip_sum = keep.astype(jnp.float32) + got.astype(jnp.float32)
    mine = lax.dynamic_index_in_dim(chip_sum, my_hi, 1, keepdims=False)
    other = lax.dynamic_index_in_dim(chip_sum, 1 - my_hi, 1, keepdims=False)
    got2 = lax.ppermute(
        other.astype(jnp.bfloat16), "tensor", [(t, t ^ 2) for t in range(n_tensor)]
    )
    output = (mine + got2.astype(jnp.float32)).astype(jnp.bfloat16)


    pair = jnp.stack([q_h, d_h])
    stats = jnp.stack([log_total[:, 0], delta])
    hi = lax.reduce_precision(stats, exponent_bits=8, mantissa_bits=7)
    rest = stats - hi
    mid = lax.reduce_precision(rest, exponent_bits=8, mantissa_bits=7)
    lo = rest - mid
    split = jnp.concatenate([hi, mid, lo]).astype(jnp.bfloat16)
    n_stat_rows = split.size // HD
    packed = jnp.concatenate(
        [pair.reshape(-1, HD), split.reshape(n_stat_rows, HD)], axis=0
    )
    pair_pieces = [pair]
    stat_pieces = [stats]
    for m in range(1, reach + 1):
        got = shifted(packed, "grp", -m)
        pair_pieces.append(got[: pair.size // HD].reshape(pair.shape))
        parts3 = got[pair.size // HD :].reshape(3, 2, blk).astype(jnp.float32)
        stat_pieces.append((parts3[0] + parts3[1]) + parts3[2])
    valid = limit - my_grp * blk
    acc0 = jnp.zeros((blk, HD), jnp.float32)
    dk_own, dv_own = key_side(
        jnp.stack([0, valid]).astype(jnp.int32), q_h, d_h, stats, k_h, v_h,
        acc0, acc0, jnp.float32, qblk=blk,
    )
    later = jnp.concatenate(pair_pieces[1:], axis=1)
    later_stats = jnp.concatenate(stat_pieces[1:], axis=1)
    dk_h, dv_h = key_side(
        jnp.stack([blk, valid]).astype(jnp.int32), later[0], later[1], later_stats, k_h, v_h,
        dk_own, dv_own, jnp.bfloat16, qblk=blk,
    )

    grads = lax.all_to_all(jnp.stack([dk_h, dv_h]), "sub", 1, 2, tiled=True)
    return (output, d_queries, grads[0], grads[1])


def solution(mesh):
    n_seq, n_tensor = mesh.devices.shape
    heads_dev = 2048 // HD // n_tensor
    regrouped = Mesh(
        mesh.devices.reshape(n_seq // heads_dev, heads_dev, n_tensor), ("grp", "sub", "tensor")
    )
    rows = P(("grp", "sub"), "tensor")
    placed = (rows, rows, rows, P("tensor", None), rows)
    return jax.shard_map(
        body,
        mesh=regrouped,
        in_specs=placed,
        out_specs=(rows, rows, rows, rows),
        check_vma=False,
    )
```

```python
import math

import jax
import jax.numpy as jnp
from jax import lax
import functools

from jax.experimental import pallas as pl
from jax.experimental.pallas import tpu as pltpu
from jax.sharding import Mesh
from jax.sharding import PartitionSpec as P

HD = 128
WINDOW = 2048


masked_score = -1e30


def shifted(block, axis, distance):
    devices = range(lax.axis_size(axis))
    route = [(i - distance, i) for i in devices if i - distance in devices]
    return lax.ppermute(block, axis, route)


def in_band(query_pos, key_pos, limit):
    return (
        (key_pos[None, :] <= query_pos[:, None])
        & (key_pos[None, :] > query_pos[:, None] - WINDOW)
        & (key_pos[None, :] >= 0)
        & (query_pos[:, None] < limit)
    )


def _kside_kernel(off_ref, q_ref, d_ref, st_ref, k_ref, v_ref, dk0_ref, dv0_ref, dk_ref, dv_ref, dk_acc, dv_acc, *, scale, qblk):
    i = pl.program_id(0)
    @pl.when(i == 0)
    def _():
        dk_acc[...] = dk0_ref[...]
        dv_acc[...] = dv0_ref[...]
    q = q_ref[...]
    d = d_ref[...]
    k = k_ref[...]
    v = v_ref[...]
    nk = k.shape[0]
    st = lax.dot_general(k, q, (((1,), (1,)), ((), ())), preferred_element_type=jnp.float32) * scale
    rk = lax.broadcasted_iota(jnp.int32, (nk, qblk), 0)
    rq = off_ref[0] + i * qblk + lax.broadcasted_iota(jnp.int32, (nk, qblk), 1)
    ok = (rk <= rq) & (rk > rq - WINDOW) & (rq < off_ref[1])
    stats = st_ref[...]
    p = jnp.where(ok, jnp.exp(st - stats[0:1, :]), 0.0)
    dp = lax.dot_general(v, d, (((1,), (1,)), ((), ())), preferred_element_type=jnp.float32)
    ds = (scale * p * (dp - stats[1:2, :])).astype(jnp.bfloat16)
    dk_acc[...] += jnp.dot(ds, q, preferred_element_type=jnp.float32)
    dv_acc[...] += jnp.dot(p.astype(jnp.bfloat16), d, preferred_element_type=jnp.float32)
    @pl.when(i == pl.num_programs(0) - 1)
    def _():
        dk_ref[...] = dk_acc[...].astype(dk_ref.dtype)
        dv_ref[...] = dv_acc[...].astype(dv_ref.dtype)

def key_side(off, later_q, later_d, stats, k_h, v_h, dk0, dv0, out_dtype, qblk=512):
    span, hd = later_q.shape
    nk = k_h.shape[0]
    scale = 1.0 / math.sqrt(HD)
    kern = functools.partial(_kside_kernel, scale=scale, qblk=qblk)
    return pl.pallas_call(
        kern,
        grid=(span // qblk,),
        in_specs=[
            pl.BlockSpec(memory_space=pltpu.SMEM),
            pl.BlockSpec((qblk, hd), lambda i: (i, 0)),
            pl.BlockSpec((qblk, hd), lambda i: (i, 0)),
            pl.BlockSpec((2, qblk), lambda i: (0, i)),
            pl.BlockSpec((nk, hd), lambda i: (0, 0)),
            pl.BlockSpec((nk, hd), lambda i: (0, 0)),
            pl.BlockSpec((nk, hd), lambda i: (0, 0)),
            pl.BlockSpec((nk, hd), lambda i: (0, 0)),
        ],
        out_specs=[pl.BlockSpec((nk, hd), lambda i: (0, 0)), pl.BlockSpec((nk, hd), lambda i: (0, 0))],
        out_shape=[jax.ShapeDtypeStruct((nk, hd), out_dtype)] * 2,
        scratch_shapes=[pltpu.VMEM((nk, hd), jnp.float32), pltpu.VMEM((nk, hd), jnp.float32)],
        compiler_params=pltpu.CompilerParams(dimension_semantics=("arbitrary",)),
    )(off, later_q, later_d, stats, k_h, v_h, dk0, dv0)


def body(query_rows, key_rows, value_rows, w_out, d_out):
    tok_rows, col_dev = query_rows.shape
    n_grp = lax.axis_size("grp")
    n_sub = lax.axis_size("sub")
    my_grp = lax.axis_index("grp")
    blk = tok_rows * n_sub
    reach = min(-(-WINDOW // blk), n_grp - 1)
    span_len = (reach + 1) * blk
    scale = 1.0 / math.sqrt(HD)
    limit = blk * n_grp
    n_tensor = lax.axis_size("tensor")
    my_t = lax.axis_index("tensor")

    qkv = lax.all_to_all(
        jnp.stack([query_rows, key_rows, value_rows]), "sub", 2, 1, tiled=True
    )
    q_h, k_h, v_h = qkv[0], qkv[1], qkv[2]

    kv = jnp.stack([k_h, v_h])
    pieces = [shifted(kv, "grp", m) for m in range(reach, 0, -1)] + [kv]
    kv_span = jnp.concatenate(pieces, axis=1)
    key_span, value_span = kv_span[0], kv_span[1]

    own_pos = my_grp * blk + jnp.arange(blk, dtype=jnp.int32)
    key_pos = (my_grp - reach) * blk + jnp.arange(span_len, dtype=jnp.int32)
    allowed = in_band(own_pos, key_pos, limit)
    scores = (
        jnp.einsum("rd,kd->rk", q_h, key_span, preferred_element_type=jnp.float32) * scale
    )
    scores = jnp.where(allowed, scores, masked_score)
    row_max = jnp.max(scores, axis=1, keepdims=True)
    log_total = row_max + jnp.log(jnp.sum(jnp.exp(scores - row_max), axis=1, keepdims=True))
    probs = jnp.where(allowed, jnp.exp(scores - log_total), 0.0)
    weights = probs.astype(jnp.bfloat16)
    att_h = jnp.einsum(
        "rk,kd->rd", weights, value_span, preferred_element_type=jnp.float32
    ).astype(jnp.bfloat16)

    far = lax.ppermute(d_out, "tensor", [(t, t ^ 2) for t in range(n_tensor)])
    near = lax.ppermute(
        jnp.stack([d_out, far]), "tensor", [(t, t ^ 1) for t in range(n_tensor)]
    )
    by_xor = jnp.stack([d_out, near[0], far, near[1]])
    order = jnp.arange(n_tensor, dtype=jnp.int32) ^ my_t
    d_out_full = jnp.moveaxis(jnp.take(by_xor, order, axis=0), 0, 1).reshape(tok_rows, -1)
    d_attended = lax.dot_general(
        d_out_full,
        w_out,
        (((1,), (1,)), ((), ())),
        preferred_element_type=jnp.float32,
    ).astype(jnp.bfloat16)
    d_h = lax.all_to_all(d_attended, "sub", 1, 0, tiled=True)
    delta = jnp.sum(d_h.astype(jnp.float32) * att_h.astype(jnp.float32), axis=1)

    d_probs = jnp.einsum("rd,kd->rk", d_h, value_span, preferred_element_type=jnp.float32)
    d_scores = (scale * probs * (d_probs - delta[:, None])).astype(jnp.bfloat16)
    dq_h = jnp.einsum(
        "rk,kd->rd", d_scores, key_span, preferred_element_type=jnp.float32
    ).astype(jnp.bfloat16)
    att_dq = lax.all_to_all(jnp.stack([att_h, dq_h]), "sub", 1, 2, tiled=True)
    attended, d_queries = att_dq[0], att_dq[1]
    partial_out = jnp.dot(attended, w_out, preferred_element_type=jnp.float32)
    my_core = my_t % 2
    my_hi = my_t // 2
    parts = partial_out.astype(jnp.bfloat16).reshape(tok_rows, n_tensor // 2, 2, -1)
    keep = lax.dynamic_index_in_dim(parts, my_core, 2, keepdims=False)
    send = lax.dynamic_index_in_dim(parts, 1 - my_core, 2, keepdims=False)
    got = lax.ppermute(send, "tensor", [(t, t ^ 1) for t in range(n_tensor)])
    chip_sum = keep.astype(jnp.float32) + got.astype(jnp.float32)
    mine = lax.dynamic_index_in_dim(chip_sum, my_hi, 1, keepdims=False)
    other = lax.dynamic_index_in_dim(chip_sum, 1 - my_hi, 1, keepdims=False)
    got2 = lax.ppermute(
        other.astype(jnp.bfloat16), "tensor", [(t, t ^ 2) for t in range(n_tensor)]
    )
    output = (mine + got2.astype(jnp.float32)).astype(jnp.bfloat16)


    pair = jnp.stack([q_h, d_h])
    stats = jnp.stack([log_total[:, 0], delta])
    hi = lax.reduce_precision(stats, exponent_bits=8, mantissa_bits=7)
    rest = stats - hi
    mid = lax.reduce_precision(rest, exponent_bits=8, mantissa_bits=7)
    lo = rest - mid
    split = jnp.concatenate([hi, mid, lo]).astype(jnp.bfloat16)
    n_stat_rows = split.size // HD
    packed = jnp.concatenate(
        [pair.reshape(-1, HD), split.reshape(n_stat_rows, HD)], axis=0
    )
    pair_pieces = [pair]
    stat_pieces = [stats]
    for m in range(1, reach + 1):
        got = shifted(packed, "grp", -m)
        pair_pieces.append(got[: pair.size // HD].reshape(pair.shape))
        parts3 = got[pair.size // HD :].reshape(3, 2, blk).astype(jnp.float32)
        stat_pieces.append((parts3[0] + parts3[1]) + parts3[2])
    valid = limit - my_grp * blk
    acc0 = jnp.zeros((blk, HD), jnp.float32)
    dk_own, dv_own = key_side(
        jnp.stack([0, valid]).astype(jnp.int32), q_h, d_h, stats, k_h, v_h,
        acc0, acc0, jnp.float32, qblk=blk,
    )
    later = jnp.concatenate(pair_pieces[1:], axis=1)
    later_stats = jnp.concatenate(stat_pieces[1:], axis=1)
    dk_h, dv_h = key_side(
        jnp.stack([blk, valid]).astype(jnp.int32), later[0], later[1], later_stats, k_h, v_h,
        dk_own, dv_own, jnp.bfloat16, qblk=2 * blk,
    )

    grads = lax.all_to_all(jnp.stack([dk_h, dv_h]), "sub", 1, 2, tiled=True)
    return (output, d_queries, grads[0], grads[1])


def solution(mesh):
    n_seq, n_tensor = mesh.devices.shape
    heads_dev = 2048 // HD // n_tensor
    regrouped = Mesh(
        mesh.devices.reshape(n_seq // heads_dev, heads_dev, n_tensor), ("grp", "sub", "tensor")
    )
    rows = P(("grp", "sub"), "tensor")
    placed = (rows, rows, rows, P("tensor", None), rows)
    return jax.shard_map(
        body,
        mesh=regrouped,
        in_specs=placed,
        out_specs=(rows, rows, rows, rows),
        check_vma=False,
    )
```
